32 devices in a mesh: seq: 8 (over z, x), dp: 4 (over y, core).
Axes of the slice: x: 2, y: 2, z: 4, core: 2. Of those that a mesh axis runs over, the one named last changes fastest.
Arguments:
- feats: bfloat16 [16384, 256], P(('dp', 'seq')), parts along dimension 0, may hold values from -6 to 6
- cotangent: bfloat16 [16384, 256], P(('dp', 'seq')), parts along dimension 0, may hold values from -6 to 6
- w_qkv: bfloat16 [256, 768], replicated, may hold values from -1.5 to 1.5
- w_out: bfloat16 [256, 256], replicated, may hold values from -0.375 to 0.375
- w_up: bfloat16 [256, 1024], replicated, may hold values from -0.375 to 0.375
- w_down: bfloat16 [1024, 256], replicated, may hold values from -0.1875 to 0.1875
- hilbert_src: int32 [16384], P(('dp', 'seq')), parts along dimension 0, may hold values from 0 to 4095, as said below
- z_dest: int32 [16384], P(('dp', 'seq')), parts along dimension 0, may hold values from 0 to 4095, as said below
- valid_count: int32 [32], P(('dp', 'seq')), parts along dimension 0, may hold values from 128 to 512
Outputs:
- out_feats: bfloat16 [16384, 256], P(('dp', 'seq')), parts along dimension 0
- grad_feats: bfloat16 [16384, 256], P(('dp', 'seq')), parts along dimension 0
- weight_grads: float32 [3145728], P(('dp', 'seq')), parts along dimension 0
The draws below stay inside these ranges and needn't reach their ends.
There are 4 independent parts, one for each index of `dp`. The reference program is written for one: setup_inputs(seed, part) draws one part's arguments, and reference() takes and returns one part's arrays. A program takes and returns all parts, laid end to end along the dimension named above; an argument that names none is the same for every part. Nothing has to cross between parts.
Inputs may be any that keep to these rules, and one draw needn't show every extreme that they name: `hilbert_src`: A permutation of the 4096 rows. The 512 positions of one Hilbert-order shard take at most 128 rows from any one z-order shard of 512 rows; every z-order shard sends exactly 128 rows to some Hilbert-order shard, and that shard receives them. `z_dest`: the inverse permutation of hilbert_src.
All inputs are finite; a program needn't handle non-finite values.
Results may differ from the reference program's by a relative error of at most 0.018.
The reference program's roundings to bfloat16 on the way count: a program that leaves them out, or rounds other values in their place, can miss the bound.
Values may be sent and summed in bfloat16 or wider, within the bound.
A program may use at most 64 MiB of HBM per device.

```python
import math
import jax
import jax.numpy as jnp
from jax import lax

C = 256
HEADS = 16
HID = 1024
PATCH = 512
R_DEV = 512
SHARDS = 8
NPTS = 4096


def shard_perm(key):
    return jax.random.permutation(key, R_DEV).astype(jnp.int32)


def route_tables(key):
    folded = jax.random.fold_in(key, 5)
    key_offset = jax.random.fold_in(folded, 1)
    key_rows = jax.random.fold_in(folded, 2)
    key_slots = jax.random.fold_in(folded, 3)
    shard_ids = jnp.arange(SHARDS, dtype=jnp.int32)
    portion = R_DEV // SHARDS
    band = min(8, SHARDS // 4)
    half_band = band // 2
    far_count = SHARDS - band
    near = (shard_ids < half_band) | (shard_ids >= SHARDS - half_band)
    far_rank = jax.random.permutation(key_offset, far_count).astype(jnp.int32)
    far_index = jnp.clip(shard_ids - half_band, 0, far_count - 1)
    empty = jnp.logical_not(near) & (far_rank[far_index] < band)
    profile = jnp.where(near, 2 * portion, jnp.where(empty, 0, portion)).astype(jnp.int32)
    counts = profile[(shard_ids[None, :] - shard_ids[:, None]) % SHARDS]
    send_end = jnp.cumsum(counts, axis=1)
    send_start = send_end - counts
    recv_start = jnp.cumsum(counts, axis=0) - counts
    local_rows = jnp.arange(R_DEV, dtype=jnp.int32)

    def find_target(ends):
        return jnp.searchsorted(ends, local_rows, side='right').astype(jnp.int32)
    targets = jax.vmap(find_target)(send_end)
    row_perm = jax.vmap(shard_perm)(jax.random.split(key_rows, SHARDS))
    position = targets * R_DEV + jnp.take_along_axis(recv_start, targets, axis=1) + local_rows[None, :] - jnp.take_along_axis(send_start, targets, axis=1)
    source = shard_ids[:, None] * R_DEV + row_perm
    table = jnp.zeros((NPTS,), jnp.int32).at[position.reshape(-1)].set(source.reshape(-1))
    shuffle = jax.vmap(shard_perm)(jax.random.split(key_slots, SHARDS))
    table = jnp.take_along_axis(table.reshape(SHARDS, R_DEV), shuffle, axis=1).reshape(-1)
    inverse = jnp.zeros((NPTS,), jnp.int32).at[table].set(jnp.arange(NPTS, dtype=jnp.int32))
    return (table, inverse)


def draw_hilbert_src(key, part):
    return route_tables(key)[0]


def draw_z_dest(key, part):
    return route_tables(key)[1]


def draw_w_qkv(key, part):
    key_base = jax.random.fold_in(jax.random.fold_in(key, 11), 0)
    weights = jax.random.truncated_normal(key_base, -4.0, 4.0, (C, 3 * C), jnp.float32) * C ** (-0.5)
    return weights.astype(jnp.bfloat16)


def plant(values, rng, low, top_value):
    longest = values.shape.index(max(values.shape))
    spots = []
    for shift in (0, 1):
        where = [jax.random.randint(jax.random.fold_in(rng, axis), (), 0, length) for axis, length in enumerate(values.shape)]
        where[longest] = (where[longest] + shift) % values.shape[longest]
        spots.append(tuple(where))
    return values.at[spots[0]].set(low).at[spots[1]].set(top_value)


def shard_levels(own_key, dims, cuts, low, top_value):
    def one(dim, parts):
        steps = jax.random.uniform(jax.random.fold_in(jax.random.fold_in(own_key, 6), dim), (parts,), jnp.float32, low / len(cuts), top_value / len(cuts))
        return jnp.repeat(jnp.exp(steps), dims[dim] // parts).reshape((-1,) + (1,) * (len(dims) - dim - 1))

    loudness = one(*cuts[0])
    for cut in cuts[1:]:
        loudness = loudness * one(*cut)
    return loudness


def centred(own_key, dims, deviation, reach, cuts=(), held_as=jnp.bfloat16):
    drawn = deviation * jax.random.normal(own_key, dims, jnp.float32)
    if cuts:
        drawn = drawn * shard_levels(own_key, dims, cuts, -0.22, 0.18)
    return jnp.clip(drawn, -reach, reach).astype(held_as)


def setup_inputs(seed: int = 0, part: int = 0) -> dict:
    key_list = jax.random.split(jax.random.key(seed), 10)
    part_splits = jax.random.split(jax.random.fold_in(key_list[9], part), 10)
    feats = centred(part_splits[0], (NPTS, C), 1.0, 6.0, ((0, 8),))
    cotangent = centred(part_splits[1], (NPTS, C), 1.0, 6.0, ((0, 8),))
    w_qkv = draw_w_qkv(jax.random.fold_in(key_list[9], 71), part)
    w_out = centred(key_list[3], (C, C), C ** -0.5, 0.375)
    w_up = centred(key_list[4], (C, HID), C ** -0.5, 0.375)
    w_down = centred(key_list[5], (HID, C), HID ** -0.5, 0.1875)
    hilbert_src = draw_hilbert_src(jax.random.fold_in(jax.random.fold_in(key_list[9], part), 71), part)
    z_dest = draw_z_dest(jax.random.fold_in(jax.random.fold_in(key_list[9], part), 71), part)
    valid_count = plant(jax.random.randint(part_splits[8], (SHARDS,), R_DEV // 4, R_DEV + 1), jax.random.fold_in(part_splits[8], 1), R_DEV // 4, R_DEV).astype(jnp.int32)
    return dict(feats=feats, cotangent=cotangent, w_qkv=w_qkv, w_out=w_out, w_up=w_up, w_down=w_down, hilbert_src=hilbert_src, z_dest=z_dest, valid_count=valid_count)


def layer_norm(inputs):
    floats = inputs.astype(jnp.float32)
    center = lax.optimization_barrier(jnp.mean(floats, axis=-1, keepdims=True))
    spread = lax.optimization_barrier(jnp.mean((floats - center) ** 2, axis=-1, keepdims=True))
    return (floats - center) * lax.rsqrt(spread + 1e-05)

def norm_back(inputs, upstream):
    floats = inputs.astype(jnp.float32)
    center = lax.optimization_barrier(jnp.mean(floats, axis=-1, keepdims=True))
    spread = lax.optimization_barrier(jnp.mean((floats - center) ** 2, axis=-1, keepdims=True))
    scale_inv = lax.rsqrt(spread + 1e-05)
    normal_part = (floats - center) * scale_inv
    first = lax.optimization_barrier(jnp.mean(upstream, axis=-1, keepdims=True))
    second = lax.optimization_barrier(jnp.mean(upstream * normal_part, axis=-1, keepdims=True))
    return scale_inv * (upstream - first - normal_part * second)

def right_dot(left, right):
    return jnp.dot(left, right, preferred_element_type=jnp.float32)

def inner_dot(left, right):
    return lax.dot_general(left, right, (((0,), (0,)), ((), ())), preferred_element_type=jnp.float32)

def back_dot(left, right):
    return lax.dot_general(left, right, (((1,), (1,)), ((), ())), preferred_element_type=jnp.float32)

def attend(query, keys, values, key_bias):
    factor = query.shape[-1] ** (-0.5)
    scores = jnp.einsum('phd,qhd->hpq', query.astype(jnp.float32), keys.astype(jnp.float32)) * factor
    scores = scores + key_bias[None, None, :]
    highest = lax.optimization_barrier(jnp.max(scores, axis=-1, keepdims=True))
    weights = jnp.exp(scores - highest)
    probs = (weights / lax.optimization_barrier(jnp.sum(weights, axis=-1, keepdims=True))).astype(jnp.bfloat16)
    mixed = jnp.einsum('hpq,qhd->phd', probs.astype(jnp.float32), values.astype(jnp.float32))
    return mixed.astype(jnp.bfloat16)

def split_heads(packed, patch, heads):
    total = packed.shape[0]
    group_heads = math.gcd(4, heads)
    head_dim = packed.shape[1] // (3 * heads)
    shaped = packed.reshape(total // patch, patch, 3, heads // group_heads, group_heads, head_dim)
    return jnp.transpose(shaped, (0, 3, 2, 1, 4, 5))

def key_biases(keep_mask, patch):
    return jnp.where(keep_mask, 0.0, -1000000000.0).astype(jnp.float32).reshape(-1, patch)

def attend_all(packed, keep_mask, patch, heads):
    tiles = split_heads(packed, patch, heads)
    biases = key_biases(keep_mask, patch)

    def per_patch(item):
        tile, bias_row = item

        def per_group(group):
            return attend(group[0], group[1], group[2], bias_row)
        return lax.map(per_group, tile)
    mixed = lax.map(per_patch, (tiles, biases))
    return jnp.transpose(mixed, (0, 2, 1, 3, 4)).reshape(packed.shape[0], packed.shape[1] // 3)

def attend_back(packed, keep_mask, upstream, patch, heads):
    tiles = split_heads(packed, patch, heads)
    biases = key_biases(keep_mask, patch)
    total = packed.shape[0]
    group_heads = math.gcd(4, heads)
    head_dim = packed.shape[1] // (3 * heads)
    up_tiles = upstream.reshape(total // patch, patch, heads // group_heads, group_heads, head_dim)
    up_tiles = jnp.transpose(up_tiles, (0, 2, 1, 3, 4))

    def per_patch(item):
        tile, up_tile, bias_row = item

        def per_group(couple):
            group, up_group = couple

            def local_attend(query, keys, values):
                return attend(query, keys, values, bias_row)
            _, pullback = jax.vjp(local_attend, group[0], group[1], group[2])
            return jnp.stack(pullback(up_group))
        return lax.map(per_group, (tile, up_tile))
    grads = lax.map(per_patch, (tiles, up_tiles, biases))
    return jnp.transpose(grads, (0, 3, 2, 1, 4, 5)).reshape(total, packed.shape[1])

def forward_rows(moved, keep_mask, w_qkv, w_out, w_up, w_down, patch, heads):
    keep_col = keep_mask.astype(jnp.float32)[:, None]
    normed = layer_norm(moved).astype(jnp.bfloat16)
    packed = right_dot(normed, w_qkv).astype(jnp.bfloat16)
    mixed = attend_all(packed, keep_mask, patch, heads)
    hidden_state = (moved.astype(jnp.float32) + keep_col * right_dot(mixed, w_out)).astype(jnp.bfloat16)
    normed_two = layer_norm(hidden_state).astype(jnp.bfloat16)
    pre_act = right_dot(normed_two, w_up)
    activated = jax.nn.gelu(pre_act).astype(jnp.bfloat16)
    result = (hidden_state.astype(jnp.float32) + keep_col * right_dot(activated, w_down)).astype(jnp.bfloat16)
    return (result, (moved, keep_mask, normed, packed, mixed, hidden_state, normed_two, pre_act, activated))

def backward_rows(saved, grad_moved, w_qkv, w_out, w_up, w_down, patch, heads):
    moved, keep_mask, normed, packed, mixed, hidden_state, normed_two, pre_act, activated = saved
    keep_col = keep_mask.astype(jnp.float32)[:, None]
    branch_two = (keep_col * grad_moved.astype(jnp.float32)).astype(jnp.bfloat16)
    grad_down = inner_dot(activated, branch_two)
    _, gelu_pull = jax.vjp(jax.nn.gelu, pre_act)
    d_pre = gelu_pull(back_dot(branch_two, w_down))[0].astype(jnp.bfloat16)
    grad_up = inner_dot(normed_two, d_pre)
    d_hidden = (grad_moved.astype(jnp.float32) + norm_back(hidden_state, back_dot(d_pre, w_up))).astype(jnp.bfloat16)
    branch_one = (keep_col * d_hidden.astype(jnp.float32)).astype(jnp.bfloat16)
    grad_out = inner_dot(mixed, branch_one)
    d_mixed = back_dot(branch_one, w_out).astype(jnp.bfloat16)
    d_packed = attend_back(packed, keep_mask, d_mixed, patch, heads)
    grad_qkv = inner_dot(normed, d_packed)
    d_moved = (d_hidden.astype(jnp.float32) + norm_back(moved, back_dot(d_packed, w_qkv))).astype(jnp.bfloat16)
    return (d_moved, (grad_qkv, grad_out, grad_up, grad_down))

def reference(feats, cotangent, w_qkv, w_out, w_up, w_down, hilbert_src, z_dest, valid_count):
    moved = feats[hilbert_src].reshape(SHARDS, R_DEV, C)
    grad_moved = cotangent[hilbert_src].reshape(SHARDS, R_DEV, C)
    keep_all = jnp.arange(R_DEV, dtype=jnp.int32)[None, :] < valid_count[:, None]
    start_sums = (jnp.zeros(w_qkv.shape, jnp.float32), jnp.zeros(w_out.shape, jnp.float32), jnp.zeros(w_up.shape, jnp.float32), jnp.zeros(w_down.shape, jnp.float32))

    def shard_step(totals, item):
        block, grad_block, keep_block = item
        result, saved = forward_rows(block, keep_block, w_qkv, w_out, w_up, w_down, PATCH, HEADS)
        d_block, grads = backward_rows(saved, grad_block, w_qkv, w_out, w_up, w_down, PATCH, HEADS)
        totals = tuple((total + grad for total, grad in zip(totals, grads)))
        return (totals, (result, d_block))
    totals, (results, d_moved) = lax.scan(shard_step, start_sums, (moved, grad_moved, keep_all))
    out_feats = results.reshape(NPTS, C)[z_dest]
    grad_feats = d_moved.reshape(NPTS, C)[z_dest]
    weight_grads = jnp.concatenate([total.reshape(-1) for total in totals])
    return (out_feats, grad_feats, weight_grads)
```

```python
import functools
import math

import jax
import jax.numpy as jnp
from jax import lax
from jax.experimental import pallas as pl
from jax.experimental.pallas import tpu as pltpu
from jax.sharding import PartitionSpec as P

HEADS = 16
F32 = jnp.float32
BF16 = jnp.bfloat16
LANES = 128
BUNCH = 4
BEFORE_LAST = 8
AFTER_LAST = 9
AT_END = 10
FAR_AT = ((1, 9, 9), (3, 10, 10))
HALF_AT = ((9, 9), (10, 10))
MESH = pl.DeviceIdType.MESH


def mm(left, right):
    return lax.dot_general(left, right, (((1,), (0,)), ((), ())), preferred_element_type=F32)


def mm_t(left, right):
    return lax.dot_general(left, right, (((1,), (1,)), ((), ())), preferred_element_type=F32)


def norm_parts(floats):
    center = jnp.mean(floats, axis=0, keepdims=True)
    gap = floats - center
    spread = jnp.mean(gap * gap, axis=0, keepdims=True)
    inverse = lax.rsqrt(spread + 1e-05)
    return gap * inverse, inverse


def norm_back(floats, upstream):
    normal, inverse = norm_parts(floats)
    first = jnp.mean(upstream, axis=0, keepdims=True)
    second = jnp.mean(upstream * normal, axis=0, keepdims=True)
    return inverse * (upstream - first - normal * second)


def column_of(row):
    return jnp.transpose(jnp.broadcast_to(row, (LANES, row.shape[1])))[:, :1]


def one_hot(rows, cols, match):
    return jnp.where(match, jnp.ones((rows, cols), F32), jnp.zeros((rows, cols), F32)).astype(BF16)


def kernel(
    shards,
    slots,
    feats_far,
    cotangent_far,
    w_qkv_far,
    w_out_far,
    w_up_far,
    w_down_far,
    hilbert_src_far,
    z_dest_far,
    valid_count_far,
    out_feats,
    grad_feats,
    weight_grads,
    outbox,
    inbox,
    pack_sel,
    unpack_sel,
    land_sel,
    w_qkv_t,
    w_out_t,
    w_up_t,
    w_down_t,
    moved_s,
    normed_s,
    packed_s,
    mixed_s,
    hidden_s,
    normed_two_s,
    act_s,
    slope_s,
    weights_s,
    inverse_s,
    d_mixed_s,
    d_hidden_s,
    d_packed_s,
    flat,
    pair_out,
    pair_in,
    far_out,
    far_in,
    send_sem,
    recv_sem,
    pair_send,
    pair_recv,
    far_send,
    far_recv,
    half_pair_send,
    half_pair_recv,
    half_far_send,
    half_far_recv,
    feats,
    cotangent,
    w_qkv,
    w_out,
    w_up,
    w_down,
    hilbert_src,
    z_dest,
    valid_count,
    load_sem,
):
    me = lax.axis_index("seq")
    rows, chans = feats.shape
    heads = HEADS
    depth = chans // heads
    hid = w_up.shape[1]
    outer = shards // 2
    share = weight_grads.shape[0]
    side = lax.rem(me, 2)
    mate = me + 1 - 2 * side
    level = lax.div(me, 2)

    barrier = pltpu.get_barrier_semaphore()

    def greet(step, carry):
        peer = lax.rem(me + step, shards)
        pl.semaphore_signal(barrier, inc=1, device_id={"seq": peer}, device_id_type=MESH)
        return carry

    lax.fori_loop(1, shards, greet, 0)

    fetches = {}
    for place, (source, here) in enumerate(
        (
            (z_dest_far, z_dest),
            (feats_far, feats),
            (cotangent_far, cotangent),
            (hilbert_src_far, hilbert_src),
            (w_qkv_far, w_qkv),
            (valid_count_far, valid_count),
            (w_out_far, w_out),
            (w_up_far, w_up),
            (w_down_far, w_down),
        )
    ):
        fetches[place] = pltpu.make_async_copy(source, here, load_sem.at[place])
        fetches[place].start()

    def box(which, home, peer, device):
        return pltpu.make_async_remote_copy(
            src_ref=outbox.at[which, peer],
            dst_ref=inbox.at[which, home],
            send_sem=send_sem.at[which, peer],
            recv_sem=recv_sem.at[which, home],
            device_id={"seq": device},
            device_id_type=MESH,
        )

    def send_all(which):
        def start(step, carry):
            peer = lax.rem(me + step, shards)
            box(which, me, peer, peer).start()
            return carry

        lax.fori_loop(1, shards, start, 0)

    def land_all(which):
        def wait(step, carry):
            peer = lax.rem(me + step, shards)
            box(which, peer, peer, peer).wait_recv()
            return carry

        lax.fori_loop(1, shards, wait, 0)

    def drain(which):
        def wait(step, carry):
            peer = lax.rem(me + step, shards)
            box(which, me, peer, peer).wait_send()
            return carry

        lax.fori_loop(1, shards, wait, 0)

    def fill(which, values):
        outbox[which] = values.reshape(shards, slots, chans).astype(BF16)
        inbox[which, me] = outbox[which, me]

    def arrived(which):
        block = inbox[which]
        if slots % 16:
            return block.astype(F32).reshape(shards * slots, chans).astype(BF16)
        return block.reshape(shards * slots, chans)

    fetches[0].wait()
    z_row = z_dest[...]
    target = lax.div(z_row, jnp.full_like(z_row, rows))
    low = target * rows
    z_col = column_of(z_row)
    before = jnp.logical_and(z_col < z_row, z_col >= low)
    rank = jnp.sum(jnp.where(before, 1.0, 0.0).astype(F32), axis=0, keepdims=True)
    send_row = target * slots + rank.astype(jnp.int32)
    slot_ids = lax.broadcasted_iota(jnp.int32, (shards * slots, rows), 0)
    pack_sel[...] = one_hot(shards * slots, rows, slot_ids == send_row)
    fetches[1].wait()
    fill(0, mm(pack_sel[...], feats[...]))
    pl.semaphore_wait(barrier, shards - 1)
    send_all(0)
    fetches[2].wait()
    fill(1, mm(pack_sel[...], cotangent[...]))

    fetches[3].wait()
    h_row = hilbert_src[...]
    source = lax.div(h_row, jnp.full_like(h_row, rows))
    source_col = column_of(source)
    first_ids = lax.broadcasted_iota(jnp.int32, (rows, rows), 0)
    second_ids = lax.broadcasted_iota(jnp.int32, (rows, rows), 1)
    before = jnp.logical_and(source_col == source, first_ids < second_ids)
    rank = jnp.sum(jnp.where(before, 1.0, 0.0).astype(F32), axis=0, keepdims=True)
    land_row = source * slots + rank.astype(jnp.int32)
    land_sel[...] = one_hot(shards * slots, rows, slot_ids == land_row)
    lane_ids = lax.broadcasted_iota(jnp.int32, (rows, shards * slots), 1)
    unpack_sel[...] = one_hot(rows, shards * slots, lane_ids == column_of(send_row))

    for place in range(4, 9):
        fetches[place].wait()
    w_qkv_t[...] = jnp.transpose(w_qkv[...])
    w_out_t[...] = jnp.transpose(w_out[...])
    w_up_t[...] = jnp.transpose(w_up[...])
    w_down_t[...] = jnp.transpose(w_down[...])

    point_ids = lax.broadcasted_iota(jnp.int32, (1, rows), 1)
    kept = point_ids < valid_count[0]
    keep = jnp.where(kept, 1.0, 0.0).astype(F32)
    bias = jnp.where(kept, 0.0, -1000000000.0).astype(F32)
    row_ids = lax.broadcasted_iota(jnp.int32, (depth, rows), 0)
    bias_rows = jnp.where(row_ids == 0, jnp.broadcast_to(bias, (depth, rows)), 0.0).astype(BF16)
    one_rows = jnp.where(row_ids == 0, 1.0, 0.0).astype(BF16)
    two_rows = jnp.where(row_ids < 2, 1.0, 0.0).astype(BF16)

    land_all(0)
    send_all(1)
    moved = mm(jnp.transpose(arrived(0)), land_sel[...])
    moved_s[...] = moved.astype(BF16)
    normal, _ = norm_parts(moved)
    normed_s[...] = normal.astype(BF16)
    packed_s[...] = mm(w_qkv_t[...], normed_s[...]).astype(BF16)
    factor = depth ** (-0.5)

    def head_forward(head):
        at = pl.multiple_of(head * depth, depth)
        query = packed_s[pl.ds(at, depth), :] * jnp.asarray(factor, BF16)
        keys = packed_s[pl.ds(chans + at, depth), :]
        values = packed_s[pl.ds(2 * chans + at, depth), :]
        query_more = jnp.concatenate([query, one_rows], axis=0)
        keys_more = jnp.transpose(jnp.concatenate([keys, bias_rows], axis=0))
        values_more = jnp.concatenate([values, one_rows], axis=0)
        scores = mm(keys_more, query_more)
        highest = jnp.max(scores, axis=0, keepdims=True)
        weights = jnp.exp(scores - highest).astype(BF16)
        weights_s[head] = weights
        total = mm(values_more, weights)
        inverse = 1.0 / total[depth : depth + 1]
        inverse_s[head] = inverse
        mixed_s[pl.ds(at, depth), :] = (total[:depth] * inverse).astype(BF16)

    bunch = math.gcd(heads, BUNCH)

    def forward_bunch(step, carry):
        for place in range(bunch):
            head_forward(bunch * step + place)
        return carry

    lax.fori_loop(0, heads // bunch, forward_bunch, 0)

    hidden = moved_s[...].astype(F32) + keep * mm(w_out_t[...], mixed_s[...])
    hidden_s[...] = hidden.astype(BF16)
    normal, _ = norm_parts(hidden_s[...].astype(F32))
    normed_two_s[...] = normal.astype(BF16)
    inner = math.sqrt(2.0 / math.pi)
    piece = math.gcd(hid, LANES)

    def up_piece(step, carry):
        at = pl.multiple_of(step * piece, piece)
        pre = mm(w_up_t[pl.ds(at, piece), :], normed_two_s[...])
        square = pre * pre
        curve = jnp.tanh(inner * (pre + 0.044715 * square * pre))
        gate = 0.5 * (1.0 + curve)
        act_s[pl.ds(at, piece), :] = (pre * gate).astype(BF16)
        bend = 0.5 * (1.0 - curve * curve) * (inner * (1.0 + 3.0 * 0.044715 * square))
        slope_s[pl.ds(at, piece), :] = gate + pre * bend
        return carry

    lax.fori_loop(0, hid // piece, up_piece, 0)
    at_out = chans * 3 * chans // LANES
    at_up = at_out + chans * chans // LANES
    at_down = at_up + chans * hid // LANES
    cols_qkv = 3 * chans // LANES
    late = at_out // (2 * share)
    ready = -(-at_down // (2 * share))
    early = outer - late
    half_share = share // 2
    slab = share // cols_qkv

    def spread_flat(start, grad):
        stride = grad.shape[1] // LANES
        for col in range(stride):
            flat[pl.ds(start + col, grad.shape[0], stride=stride), :] = grad[
                :, col * LANES : (col + 1) * LANES
            ]

    def pair_copy(step):
        return pltpu.make_async_remote_copy(
            src_ref=pair_out.at[step],
            dst_ref=pair_in.at[step],
            send_sem=pair_send.at[step],
            recv_sem=pair_recv.at[step],
            device_id={"seq": mate},
            device_id_type=MESH,
        )

    def keep_bit(stage):
        return lax.rem(lax.div(level, 2**stage), 2)

    def partner(stage):
        return me + 2 ** (stage + 1) * (1 - 2 * keep_bit(stage))

    def part_of(stage, place):
        low = lax.rem(level, 2**stage)
        return low + 2**stage * (1 - keep_bit(stage)) + 2 ** (stage + 1) * place

    def far_slot(stage, part):
        return outer - outer // 2**stage + lax.div(part, 2 ** (stage + 1))

    def far_copy(stage, part):
        slot = far_slot(stage, part)
        return pltpu.make_async_remote_copy(
            src_ref=far_out.at[part],
            dst_ref=far_in.at[slot],
            send_sem=far_send.at[part],
            recv_sem=far_recv.at[slot],
            device_id={"seq": partner(stage)},
            device_id_type=MESH,
        )

    def half_rows(half):
        return pl.ds(half * half_share, half_share)

    def half_pair_copy(half, step):
        return pltpu.make_async_remote_copy(
            src_ref=pair_out.at[step, half_rows(half)],
            dst_ref=pair_in.at[step, half_rows(half)],
            send_sem=half_pair_send.at[half, step],
            recv_sem=half_pair_recv.at[half, step],
            device_id={"seq": mate},
            device_id_type=MESH,
        )

    def half_far_copy(half, stage, part):
        slot = far_slot(stage, part)
        return pltpu.make_async_remote_copy(
            src_ref=far_out.at[part, half_rows(half)],
            dst_ref=far_in.at[slot, half_rows(half)],
            send_sem=half_far_send.at[half, part],
            recv_sem=half_far_recv.at[half, slot],
            device_id={"seq": partner(stage)},
            device_id_type=MESH,
        )

    def flat_rows(step, which):
        return pl.ds(pl.multiple_of((2 * step + which) * share, 16), share)

    def flat_half(step, which, half):
        at = (2 * step + which) * share + half * half_share
        return pl.ds(pl.multiple_of(at, 8), half_share)

    def pair_start(step, carry):
        pair_out[step] = flat[flat_rows(step, 1 - side), :].astype(BF16)
        pair_copy(step).start()
        return carry

    def part_sum(stage, part):
        pair_copy(part).wait_recv()
        total = flat[flat_rows(part, side), :] + pair_in[part].astype(F32)
        for before in range(stage):
            far_copy(before, part).wait_recv()
            total = total + far_in[far_slot(before, part)].astype(F32)
        return total

    def far_start(stage, first, last):
        def start(place, carry):
            part = part_of(stage, place)

            @pl.when(jnp.logical_and(part >= first, part < last))
            def _():
                far_out[part] = part_sum(stage, part).astype(BF16)
                far_copy(stage, part).start()

            return carry

        lax.fori_loop(0, outer // 2 ** (stage + 1), start, 0)

    def half_grad(half):
        for col in range(half, cols_qkv, 2):
            grad = mm_t(normed_s[...], d_packed_s[col * LANES : (col + 1) * LANES, :])
            for shard in range(2 * late):
                at = shard * share + half * half_share + (col // 2) * slab
                flat[at : at + slab, :] = grad[shard * slab : (shard + 1) * slab]

    def half_pair_start(half):
        def start(step, carry):
            pair_out[step, half_rows(half)] = flat[flat_half(step, 1 - side, half), :].astype(BF16)
            half_pair_copy(half, step).start()
            return carry

        lax.fori_loop(0, late, start, 0)

    def half_sum(half, stage, part):
        half_pair_copy(half, part).wait_recv()
        total = flat[flat_half(part, side, half), :]
        total = total + pair_in[part, half_rows(half)].astype(F32)
        for before in range(stage):
            half_far_copy(half, before, part).wait_recv()
            total = total + far_in[far_slot(before, part), half_rows(half)].astype(F32)
        return total

    def half_far_start(half, stage):
        def start(place, carry):
            part = part_of(stage, place)

            @pl.when(part < late)
            def _():
                far_out[part, half_rows(half)] = half_sum(half, stage, part).astype(BF16)
                half_far_copy(half, stage, part).start()

            return carry

        lax.fori_loop(0, outer // 2 ** (stage + 1), start, 0)

    land_all(1)
    upstream = mm(jnp.transpose(arrived(1)), land_sel[...])
    branch = (keep * upstream).astype(BF16)
    spread_flat(at_down, mm_t(act_s[...], branch))
    lax.fori_loop(ready, outer, pair_start, 0)
    block = hidden_s[...].astype(F32) + keep * mm(w_down_t[...], act_s[...])
    fill(2, mm_t(land_sel[...], block.astype(BF16)))
    send_all(2)

    def down_piece(step, carry):
        at = pl.multiple_of(step * piece, piece)
        d_act = mm(w_down[pl.ds(at, piece), :], branch)
        act_s[pl.ds(at, piece), :] = (d_act * slope_s[pl.ds(at, piece), :]).astype(BF16)
        return carry

    lax.fori_loop(0, hid // piece, down_piece, 0)
    spread_flat(at_up, mm_t(normed_two_s[...], act_s[...]))
    d_hidden = upstream + norm_back(hidden_s[...].astype(F32), mm(w_up[...], act_s[...]))
    d_hidden_s[...] = d_hidden.astype(BF16)
    branch_one = (keep * d_hidden_s[...].astype(F32)).astype(BF16)
    spread_flat(at_out, mm_t(mixed_s[...], branch_one))
    d_mixed_s[...] = mm(w_out[...], branch_one).astype(BF16)

    def head_backward(head):
        at = pl.multiple_of(head * depth, depth)
        query = packed_s[pl.ds(at, depth), :] * jnp.asarray(factor, BF16)
        keys = packed_s[pl.ds(chans + at, depth), :]
        values = packed_s[pl.ds(2 * chans + at, depth), :]
        values_more = jnp.transpose(jnp.concatenate([values, two_rows], axis=0))
        scaled = (d_mixed_s[pl.ds(at, depth), :].astype(F32) * inverse_s[head]).astype(BF16)
        mixed = mixed_s[pl.ds(at, depth), :].astype(F32)
        delta = -jnp.sum(scaled.astype(F32) * mixed, axis=0, keepdims=True)
        coarse = delta.astype(BF16).astype(F32)
        fine = delta - coarse
        tail = jnp.where(
            row_ids == 0,
            jnp.broadcast_to(coarse, (depth, rows)),
            jnp.where(row_ids == 1, jnp.broadcast_to(fine, (depth, rows)), 0.0),
        ).astype(BF16)
        scaled_more = jnp.concatenate([scaled, tail], axis=0)
        weights = weights_s[head]
        gap = mm(values_more, scaled_more).astype(BF16)
        d_scores = weights * gap
        d_query = mm(keys, d_scores) * factor
        d_packed_s[pl.ds(at, depth), :] = d_query.astype(BF16)
        d_packed_s[pl.ds(chans + at, depth), :] = mm_t(query, d_scores).astype(BF16)
        d_packed_s[pl.ds(2 * chans + at, depth), :] = mm_t(scaled, weights).astype(BF16)

    lax.fori_loop(late, ready, pair_start, 0)

    bunches = heads // bunch

    stages = outer.bit_length() - 1
    middle = min(2 * late, ready)
    groups = ((ready, outer), (middle, ready), (late, middle))

    def relay(place):
        for stage in range(stages):
            for group, (first, last) in enumerate(groups):
                if (FAR_AT[stage][group] if stage < 2 else AT_END) == place and first < last:
                    far_start(stage, first, last)
            for half in range(2):
                if (HALF_AT[stage][half] if stage < 2 else AT_END) == place:
                    half_far_start(half, stage)

    def backward_bunch(step, carry):
        for place in range(bunch):
            head_backward(bunch * step + place)
        for place in range(bunches):
            if any(place in row for row in FAR_AT + HALF_AT):

                @pl.when(step == place)
                def _(place=place):
                    relay(place)

        @pl.when(step == bunches // 2 - 1)
        def _():
            half_grad(0)
            half_pair_start(0)

        return carry

    lax.fori_loop(0, bunches, backward_bunch, 0)
    half_grad(1)
    half_pair_start(1)
    relay(BEFORE_LAST)
    d_moved = d_hidden_s[...].astype(F32) + norm_back(
        moved_s[...].astype(F32), mm(w_qkv[...], d_packed_s[...])
    )
    fill(3, mm_t(land_sel[...], d_moved.astype(BF16)))
    send_all(3)
    relay(AFTER_LAST)

    land_all(2)
    out_feats[...] = mm(unpack_sel[...], arrived(2)).astype(BF16)

    relay(AT_END)

    @pl.when(level >= late)
    def _():
        weight_grads[...] = part_sum(stages, level)

    land_all(3)
    grad_feats[...] = mm(unpack_sel[...], arrived(3)).astype(BF16)

    @pl.when(level < late)
    def _():
        for half in range(2):
            flat[flat_half(level, side, half), :] = half_sum(half, stages, level)
        for col in range(cols_qkv):
            at = (2 * level + side) * share + (col % 2) * half_share + (col // 2) * slab
            weight_grads[pl.ds(col, slab, stride=cols_qkv), :] = flat[
                pl.ds(pl.multiple_of(at, 8), slab), :
            ]

    def pair_drain(step, carry):
        pair_copy(step).wait_send()
        return carry

    lax.fori_loop(late, outer, pair_drain, 0)

    def far_drain(stage):
        def wait(place, carry):
            part = part_of(stage, place)

            @pl.when(part >= late)
            def _():
                far_copy(stage, part).wait_send()

            @pl.when(part < late)
            def _():
                for half in range(2):
                    half_far_copy(half, stage, part).wait_send()

            return carry

        lax.fori_loop(0, outer // 2 ** (stage + 1), wait, 0)

    for stage in range(stages):
        far_drain(stage)

    def half_drain(step, carry):
        for half in range(2):
            half_pair_copy(half, step).wait_send()
        return carry

    lax.fori_loop(0, late, half_drain, 0)
    for which in range(4):
        drain(which)


def hand_over(*refs):
    count = len(refs) // 2
    sems = refs[-1]
    copies = [
        pltpu.make_async_copy(refs[place], refs[count + place], sems.at[place])
        for place in range(count)
    ]
    for copy in copies:
        copy.start()
    for copy in copies:
        copy.wait()


def body(feats, cotangent, w_qkv, w_out, w_up, w_down, hilbert_src, z_dest, valid_count):
    rows, chans = feats.shape
    hid = w_up.shape[1]
    shards = lax.axis_size("seq")
    slots = 2 * rows // shards
    outer = shards // 2
    packed = w_qkv.shape[1]
    flat_rows = (chans * packed + chans * chans + 2 * chans * hid) // LANES
    share = flat_rows // shards
    vmem = pl.BlockSpec(memory_space=pltpu.VMEM)
    dma = pltpu.SemaphoreType.DMA
    out_feats, grad_feats, weight_grads = pl.pallas_call(
        functools.partial(kernel, shards, slots),
        out_shape=(
            jax.ShapeDtypeStruct((rows, chans), BF16),
            jax.ShapeDtypeStruct((rows, chans), BF16),
            jax.ShapeDtypeStruct((share, LANES), F32),
        ),
        in_specs=[pl.BlockSpec(memory_space=pltpu.HBM)] * 9,
        out_specs=(vmem, vmem, vmem),
        scratch_shapes=[
            pltpu.VMEM((4, shards, slots, chans), BF16),
            pltpu.VMEM((4, shards, slots, chans), BF16),
            pltpu.VMEM((shards * slots, rows), BF16),
            pltpu.VMEM((rows, shards * slots), BF16),
            pltpu.VMEM((shards * slots, rows), BF16),
            pltpu.VMEM((packed, chans), BF16),
            pltpu.VMEM((chans, chans), BF16),
            pltpu.VMEM((hid, chans), BF16),
            pltpu.VMEM((chans, hid), BF16),
            pltpu.VMEM((chans, rows), BF16),
            pltpu.VMEM((chans, rows), BF16),
            pltpu.VMEM((packed, rows), BF16),
            pltpu.VMEM((chans, rows), BF16),
            pltpu.VMEM((chans, rows), BF16),
            pltpu.VMEM((chans, rows), BF16),
            pltpu.VMEM((hid, rows), BF16),
            pltpu.VMEM((hid, rows), F32),
            pltpu.VMEM((HEADS, rows, rows), BF16),
            pltpu.VMEM((HEADS, 1, rows), F32),
            pltpu.VMEM((chans, rows), BF16),
            pltpu.VMEM((chans, rows), BF16),
            pltpu.VMEM((packed, rows), BF16),
            pltpu.VMEM((flat_rows, LANES), F32),
            pltpu.VMEM((outer, share, LANES), BF16),
            pltpu.VMEM((outer, share, LANES), BF16),
            pltpu.VMEM((outer, share, LANES), BF16),
            pltpu.VMEM((outer, share, LANES), BF16),
            dma((4, shards)),
            dma((4, shards)),
            dma((outer,)),
            dma((outer,)),
            dma((outer,)),
            dma((outer,)),
            dma((2, outer)),
            dma((2, outer)),
            dma((2, outer)),
            dma((2, outer)),
            pltpu.VMEM((rows, chans), BF16),
            pltpu.VMEM((rows, chans), BF16),
            pltpu.VMEM((chans, packed), BF16),
            pltpu.VMEM((chans, chans), BF16),
            pltpu.VMEM((chans, hid), BF16),
            pltpu.VMEM((hid, chans), BF16),
            pltpu.VMEM((1, rows), jnp.int32),
            pltpu.VMEM((1, rows), jnp.int32),
            pltpu.SMEM((1,), jnp.int32),
            dma((9,)),
        ],
        compiler_params=pltpu.CompilerParams(
            collective_id=0, has_side_effects=True, vmem_limit_bytes=60 * 1024 * 1024
        ),
        name="block_step",
    )(
        feats,
        cotangent,
        w_qkv,
        w_out,
        w_up,
        w_down,
        hilbert_src.reshape(1, rows),
        z_dest.reshape(1, rows),
        valid_count,
    )
    results = (out_feats, grad_feats, weight_grads)
    far = vmem
    out_feats, grad_feats, weight_grads = pl.pallas_call(
        hand_over,
        out_shape=tuple(jax.ShapeDtypeStruct(array.shape, array.dtype) for array in results),
        in_specs=[far] * len(results),
        out_specs=(far,) * len(results),
        scratch_shapes=[dma((len(results),))],
        name="hand_over",
    )(*results)
    return out_feats, grad_feats, weight_grads.reshape(-1)


def solution(mesh):
    in_specs = (
        P(("dp", "seq"), None),
        P(("dp", "seq"), None),
        P(),
        P(),
        P(),
        P(),
        P(("dp", "seq")),
        P(("dp", "seq")),
        P(("dp", "seq")),
    )
    out_specs = (P(("dp", "seq"), None), P(("dp", "seq"), None), P(("dp", "seq")))
    return jax.shard_map(body, mesh=mesh, in_specs=in_specs, out_specs=out_specs, check_vma=False)
```

```python
import functools
import math

import jax
import jax.numpy as jnp
from jax import lax
from jax.experimental import pallas as pl
from jax.experimental.pallas import tpu as pltpu
from jax.sharding import PartitionSpec as P

HEADS = 16
F32 = jnp.float32
BF16 = jnp.bfloat16
LANES = 128
BUNCH = 4
BEFORE_LAST = 8
AFTER_LAST = 9
AT_END = 10
PLAN = {1: ((0, 0),), 3: ((1, 0),), 9: ((0, 1), (0, 2), (0, 3), (0, 4)), 10: ((1, 1), (1, 2), (1, 3), (1, 4))}
MESH = pl.DeviceIdType.MESH


def mm(left, right):
    return lax.dot_general(left, right, (((1,), (0,)), ((), ())), preferred_element_type=F32)


def mm_t(left, right):
    return lax.dot_general(left, right, (((1,), (1,)), ((), ())), preferred_element_type=F32)


def norm_parts(floats):
    center = jnp.mean(floats, axis=0, keepdims=True)
    gap = floats - center
    spread = jnp.mean(gap * gap, axis=0, keepdims=True)
    inverse = lax.rsqrt(spread + 1e-05)
    return gap * inverse, inverse


def norm_back(floats, upstream):
    normal, inverse = norm_parts(floats)
    first = jnp.mean(upstream, axis=0, keepdims=True)
    second = jnp.mean(upstream * normal, axis=0, keepdims=True)
    return inverse * (upstream - first - normal * second)


def column_of(row):
    return jnp.transpose(jnp.broadcast_to(row, (LANES, row.shape[1])))[:, :1]


def one_hot(rows, cols, match):
    return jnp.where(match, jnp.ones((rows, cols), F32), jnp.zeros((rows, cols), F32)).astype(BF16)


def kernel(
    shards,
    slots,
    feats_far,
    cotangent_far,
    w_qkv_far,
    w_out_far,
    w_up_far,
    w_down_far,
    hilbert_src_far,
    z_dest_far,
    valid_count_far,
    out_feats,
    grad_feats,
    weight_grads,
    outbox,
    inbox,
    pack_sel,
    unpack_sel,
    land_sel,
    w_qkv_t,
    w_out_t,
    w_up_t,
    w_down_t,
    moved_s,
    normed_s,
    packed_s,
    mixed_s,
    hidden_s,
    normed_two_s,
    act_s,
    slope_s,
    weights_s,
    inverse_s,
    d_mixed_s,
    d_hidden_s,
    d_packed_s,
    flat,
    pair_out,
    pair_in,
    far_out,
    far_in,
    send_sem,
    recv_sem,
    pair_send,
    pair_recv,
    far_send,
    far_recv,
    half_pair_send,
    half_pair_recv,
    half_far_send,
    half_far_recv,
    feats,
    cotangent,
    w_qkv,
    w_out,
    w_up,
    w_down,
    hilbert_src,
    z_dest,
    valid_count,
    load_sem,
):
    me = lax.axis_index("seq")
    rows, chans = feats.shape
    heads = HEADS
    depth = chans // heads
    hid = w_up.shape[1]
    outer = shards // 2
    share = weight_grads.shape[0]
    side = lax.rem(me, 2)
    mate = me + 1 - 2 * side
    level = lax.div(me, 2)

    barrier = pltpu.get_barrier_semaphore()

    def greet(step, carry):
        peer = lax.rem(me + step, shards)
        pl.semaphore_signal(barrier, inc=1, device_id={"seq": peer}, device_id_type=MESH)
        return carry

    lax.fori_loop(1, shards, greet, 0)

    fetches = {}
    for place, (source, here) in enumerate(
        (
            (z_dest_far, z_dest),
            (feats_far, feats),
            (cotangent_far, cotangent),
            (hilbert_src_far, hilbert_src),
            (w_qkv_far, w_qkv),
            (valid_count_far, valid_count),
            (w_out_far, w_out),
            (w_up_far, w_up),
            (w_down_far, w_down),
        )
    ):
        fetches[place] = pltpu.make_async_copy(source, here, load_sem.at[place])
        fetches[place].start()

    def box(which, home, peer, device):
        return pltpu.make_async_remote_copy(
            src_ref=outbox.at[which, peer],
            dst_ref=inbox.at[which, home],
            send_sem=send_sem.at[which, peer],
            recv_sem=recv_sem.at[which, home],
            device_id={"seq": device},
            device_id_type=MESH,
        )

    def send_one(which, jump):
        peer = lax.rem(me + jump, shards)
        box(which, me, peer, peer).start()

    def send_all(which):
        def start(step, carry):
            send_one(which, outer + (1 - 2 * lax.rem(step, 2)) * (step // 2))
            return carry

        lax.fori_loop(1, shards, start, 0)

    def send_odd(which, odd):
        def start(step, carry):
            @pl.when(lax.rem(outer + (1 - 2 * lax.rem(step, 2)) * (step // 2), 2) == odd)
            def _():
                send_one(which, outer + (1 - 2 * lax.rem(step, 2)) * (step // 2))

            return carry

        lax.fori_loop(1, shards, start, 0)

    def land_all(which):
        def wait(step, carry):
            peer = lax.rem(me + step, shards)
            box(which, peer, peer, peer).wait_recv()
            return carry

        lax.fori_loop(1, shards, wait, 0)

    def drain(which):
        def wait(step, carry):
            peer = lax.rem(me + step, shards)
            box(which, me, peer, peer).wait_send()
            return carry

        lax.fori_loop(1, shards, wait, 0)

    def fill(which, values):
        outbox[which] = values.reshape(shards, slots, chans).astype(BF16)
        inbox[which, me] = outbox[which, me]

    def arrived(which):
        block = inbox[which]
        if slots % 16:
            return block.astype(F32).reshape(shards * slots, chans).astype(BF16)
        return block.reshape(shards * slots, chans)

    fetches[0].wait()
    z_row = z_dest[...]
    target = lax.div(z_row, jnp.full_like(z_row, rows))
    low = target * rows
    z_col = column_of(z_row)
    before = jnp.logical_and(z_col < z_row, z_col >= low)
    rank = jnp.sum(jnp.where(before, 1.0, 0.0).astype(F32), axis=0, keepdims=True)
    send_row = target * slots + rank.astype(jnp.int32)
    slot_ids = lax.broadcasted_iota(jnp.int32, (shards * slots, rows), 0)
    pack_sel[...] = one_hot(shards * slots, rows, slot_ids == send_row)
    fetches[1].wait()
    fill(0, mm(pack_sel[...], feats[...]))
    pl.semaphore_wait(barrier, shards - 1)
    send_all(0)
    fetches[2].wait()
    fill(1, mm(pack_sel[...], cotangent[...]))

    fetches[3].wait()
    h_row = hilbert_src[...]
    source = lax.div(h_row, jnp.full_like(h_row, rows))
    source_col = column_of(source)
    first_ids = lax.broadcasted_iota(jnp.int32, (rows, rows), 0)
    second_ids = lax.broadcasted_iota(jnp.int32, (rows, rows), 1)
    before = jnp.logical_and(source_col == source, first_ids < second_ids)
    rank = jnp.sum(jnp.where(before, 1.0, 0.0).astype(F32), axis=0, keepdims=True)
    land_row = source * slots + rank.astype(jnp.int32)
    land_sel[...] = one_hot(shards * slots, rows, slot_ids == land_row)
    lane_ids = lax.broadcasted_iota(jnp.int32, (rows, shards * slots), 1)
    unpack_sel[...] = one_hot(rows, shards * slots, lane_ids == column_of(send_row))

    for place in range(4, 9):
        fetches[place].wait()
    w_qkv_t[...] = jnp.transpose(w_qkv[...])
    w_out_t[...] = jnp.transpose(w_out[...])
    w_up_t[...] = jnp.transpose(w_up[...])
    w_down_t[...] = jnp.transpose(w_down[...])

    point_ids = lax.broadcasted_iota(jnp.int32, (1, rows), 1)
    kept = point_ids < valid_count[0]
    keep = jnp.where(kept, 1.0, 0.0).astype(F32)
    bias = jnp.where(kept, 0.0, -1000000000.0).astype(F32)
    row_ids = lax.broadcasted_iota(jnp.int32, (depth, rows), 0)
    bias_rows = jnp.where(row_ids == 0, jnp.broadcast_to(bias, (depth, rows)), 0.0).astype(BF16)
    one_rows = jnp.where(row_ids == 0, 1.0, 0.0).astype(BF16)
    two_rows = jnp.where(row_ids < 2, 1.0, 0.0).astype(BF16)

    land_all(0)
    send_all(1)
    moved = mm(jnp.transpose(arrived(0)), land_sel[...])
    moved_s[...] = moved.astype(BF16)
    normal, _ = norm_parts(moved)
    normed_s[...] = normal.astype(BF16)
    packed_s[...] = mm(w_qkv_t[...], normed_s[...]).astype(BF16)
    factor = depth ** (-0.5)

    def head_forward(head):
        at = pl.multiple_of(head * depth, depth)
        query = packed_s[pl.ds(at, depth), :] * jnp.asarray(factor, BF16)
        keys = packed_s[pl.ds(chans + at, depth), :]
        values = packed_s[pl.ds(2 * chans + at, depth), :]
        query_more = jnp.concatenate([query, one_rows], axis=0)
        keys_more = jnp.transpose(jnp.concatenate([keys, bias_rows], axis=0))
        values_more = jnp.concatenate([values, one_rows], axis=0)
        scores = mm(keys_more, query_more)
        highest = jnp.max(scores, axis=0, keepdims=True)
        weights = jnp.exp(scores - highest).astype(BF16)
        weights_s[head] = weights
        total = mm(values_more, weights)
        inverse = 1.0 / total[depth : depth + 1]
        inverse_s[head] = inverse
        mixed_s[pl.ds(at, depth), :] = (total[:depth] * inverse).astype(BF16)

    bunch = math.gcd(heads, BUNCH)

    def forward_bunch(step, carry):
        for place in range(bunch):
            head_forward(bunch * step + place)
        return carry

    lax.fori_loop(0, heads // bunch, forward_bunch, 0)

    hidden = moved_s[...].astype(F32) + keep * mm(w_out_t[...], mixed_s[...])
    hidden_s[...] = hidden.astype(BF16)
    normal, _ = norm_parts(hidden_s[...].astype(F32))
    normed_two_s[...] = normal.astype(BF16)
    inner = math.sqrt(2.0 / math.pi)
    piece = math.gcd(hid, LANES)

    def up_piece(step, carry):
        at = pl.multiple_of(step * piece, piece)
        pre = mm(w_up_t[pl.ds(at, piece), :], normed_two_s[...])
        curve = jnp.tanh(inner * (pre + 0.044715 * pre * pre * pre))
        act_s[pl.ds(at, piece), :] = (pre * (0.5 * (1.0 + curve))).astype(BF16)
        slope_s[pl.ds(at, piece), :] = pre
        return carry

    lax.fori_loop(0, hid // piece, up_piece, 0)
    at_out = chans * 3 * chans // LANES
    at_up = at_out + chans * chans // LANES
    at_down = at_up + chans * hid // LANES
    cols_qkv = 3 * chans // LANES
    late = at_out // (2 * share)
    ready = -(-at_down // (2 * share))
    early = outer - late
    half_share = share // 2
    stages = outer.bit_length() - 1
    middle = min(2 * late, ready)
    slab = share // cols_qkv

    def spread_flat(start, grad):
        stride = grad.shape[1] // LANES
        for col in range(stride):
            flat[pl.ds(start + col, grad.shape[0], stride=stride), :] = grad[
                :, col * LANES : (col + 1) * LANES
            ]

    def pair_copy(step):
        return pltpu.make_async_remote_copy(
            src_ref=pair_out.at[step],
            dst_ref=pair_in.at[step],
            send_sem=pair_send.at[step],
            recv_sem=pair_recv.at[step],
            device_id={"seq": mate},
            device_id_type=MESH,
        )

    def keep_bit(stage):
        return lax.rem(lax.div(level, 2**stage), 2)

    def partner(stage):
        return me + 2 ** (stage + 1) * (1 - 2 * keep_bit(stage))

    def part_of(stage, place):
        low = lax.rem(level, 2**stage)
        return low + 2**stage * (1 - keep_bit(stage)) + 2 ** (stage + 1) * place

    def far_slot(stage, part):
        return outer - outer // 2**stage + lax.div(part, 2 ** (stage + 1))

    def far_copy(stage, part):
        slot = far_slot(stage, part)
        return pltpu.make_async_remote_copy(
            src_ref=far_out.at[part],
            dst_ref=far_in.at[slot],
            send_sem=far_send.at[part],
            recv_sem=far_recv.at[slot],
            device_id={"seq": partner(stage)},
            device_id_type=MESH,
        )

    def half_rows(half):
        return pl.ds(half * half_share, half_share)

    def half_pair_copy(half, step):
        return pltpu.make_async_remote_copy(
            src_ref=pair_out.at[step, half_rows(half)],
            dst_ref=pair_in.at[step, half_rows(half)],
            send_sem=half_pair_send.at[half, step],
            recv_sem=half_pair_recv.at[half, step],
            device_id={"seq": mate},
            device_id_type=MESH,
        )

    def half_far_copy(half, stage, part):
        slot = far_slot(stage, part)
        return pltpu.make_async_remote_copy(
            src_ref=far_out.at[part, half_rows(half)],
            dst_ref=far_in.at[slot, half_rows(half)],
            send_sem=half_far_send.at[half, part],
            recv_sem=half_far_recv.at[half, slot],
            device_id={"seq": partner(stage)},
            device_id_type=MESH,
        )

    def flat_rows(step, which):
        return pl.ds(pl.multiple_of((2 * step + which) * share, 16), share)

    def flat_half(step, which, half):
        at = (2 * step + which) * share + half * half_share
        return pl.ds(pl.multiple_of(at, 8), half_share)

    def pair_start(step, carry):
        pair_out[step] = flat[flat_rows(step, 1 - side), :].astype(BF16)
        pair_copy(step).start()
        return carry

    def part_sum(stage, part):
        pair_copy(part).wait_recv()
        total = flat[flat_rows(part, side), :] + pair_in[part].astype(F32)
        for before in range(stage):
            far_copy(before, part).wait_recv()
            total = total + far_in[far_slot(before, part)].astype(F32)
        return total

    def far_start(stage, first, last):
        def start(place, carry):
            part = part_of(stage, place)

            @pl.when(jnp.logical_and(part >= first, part < last))
            def _():
                far_out[part] = part_sum(stage, part).astype(BF16)
                far_copy(stage, part).start()

            return carry

        lax.fori_loop(0, outer // 2 ** (stage + 1), start, 0)

    def half_grad(half):
        for col in range(half, cols_qkv, 2):
            grad = mm_t(normed_s[...], d_packed_s[col * LANES : (col + 1) * LANES, :])
            for shard in range(2 * late):
                at = shard * share + half * half_share + (col // 2) * slab
                flat[at : at + slab, :] = grad[shard * slab : (shard + 1) * slab]

    def half_pair_start(half):
        def start(step, carry):
            pair_out[step, half_rows(half)] = flat[flat_half(step, 1 - side, half), :].astype(BF16)
            half_pair_copy(half, step).start()
            return carry

        lax.fori_loop(0, late, start, 0)

    def half_sum(half, stage, part):
        half_pair_copy(half, part).wait_recv()
        total = flat[flat_half(part, side, half), :]
        total = total + pair_in[part, half_rows(half)].astype(F32)
        for before in range(stage):
            half_far_copy(half, before, part).wait_recv()
            total = total + far_in[far_slot(before, part), half_rows(half)].astype(F32)
        return total

    def half_far_start(half, stage):
        def start(place, carry):
            part = part_of(stage, place)

            @pl.when(part < late)
            def _():
                far_out[part, half_rows(half)] = half_sum(half, stage, part).astype(BF16)
                half_far_copy(half, stage, part).start()

            return carry

        lax.fori_loop(0, outer // 2 ** (stage + 1), start, 0)

    land_all(1)
    upstream = mm(jnp.transpose(arrived(1)), land_sel[...])
    branch = (keep * upstream).astype(BF16)
    spread_flat(at_down, mm_t(act_s[...], branch))
    lax.fori_loop(ready, outer, pair_start, 0)
    block = hidden_s[...].astype(F32) + keep * mm(w_down_t[...], act_s[...])
    fill(2, mm_t(land_sel[...], block.astype(BF16)))
    send_all(2)

    def down_piece(step, carry):
        at = pl.multiple_of(step * piece, piece)
        d_act = mm(w_down[pl.ds(at, piece), :], branch)
        pre = slope_s[pl.ds(at, piece), :]
        square = pre * pre
        curve = jnp.tanh(inner * (pre + 0.044715 * square * pre))
        bend = 0.5 * (1.0 - curve * curve) * (inner * (1.0 + 3.0 * 0.044715 * square))
        slope = 0.5 * (1.0 + curve) + pre * bend
        act_s[pl.ds(at, piece), :] = (d_act * slope).astype(BF16)
        return carry

    lax.fori_loop(0, hid // piece, down_piece, 0)
    spread_flat(at_up, mm_t(normed_two_s[...], act_s[...]))
    d_hidden = upstream + norm_back(hidden_s[...].astype(F32), mm(w_up[...], act_s[...]))
    d_hidden_s[...] = d_hidden.astype(BF16)
    branch_one = (keep * d_hidden_s[...].astype(F32)).astype(BF16)
    spread_flat(at_out, mm_t(mixed_s[...], branch_one))
    d_mixed_s[...] = mm(w_out[...], branch_one).astype(BF16)

    def head_backward(head):
        at = pl.multiple_of(head * depth, depth)
        query = packed_s[pl.ds(at, depth), :] * jnp.asarray(factor, BF16)
        keys = packed_s[pl.ds(chans + at, depth), :]
        values = packed_s[pl.ds(2 * chans + at, depth), :]
        values_more = jnp.transpose(jnp.concatenate([values, two_rows], axis=0))
        scaled = (d_mixed_s[pl.ds(at, depth), :].astype(F32) * inverse_s[head]).astype(BF16)
        mixed = mixed_s[pl.ds(at, depth), :].astype(F32)
        delta = -jnp.sum(scaled.astype(F32) * mixed, axis=0, keepdims=True)
        coarse = delta.astype(BF16).astype(F32)
        fine = delta - coarse
        tail = jnp.where(
            row_ids == 0,
            jnp.broadcast_to(coarse, (depth, rows)),
            jnp.where(row_ids == 1, jnp.broadcast_to(fine, (depth, rows)), 0.0),
        ).astype(BF16)
        scaled_more = jnp.concatenate([scaled, tail], axis=0)
        weights = weights_s[head]
        gap = mm(values_more, scaled_more).astype(BF16)
        d_scores = weights * gap
        d_query = mm(keys, d_scores) * factor
        d_packed_s[pl.ds(at, depth), :] = d_query.astype(BF16)
        d_packed_s[pl.ds(chans + at, depth), :] = mm_t(query, d_scores).astype(BF16)
        d_packed_s[pl.ds(2 * chans + at, depth), :] = mm_t(scaled, weights).astype(BF16)

    lax.fori_loop(late, ready, pair_start, 0)

    bunches = heads // bunch

    groups = ((ready, outer), (middle, ready), (late, middle))

    def relay(place):
        for stage, group in PLAN.get(place, ()):
            for step in (stage,) if stage == 0 else range(stage, stages):
                if group < len(groups):
                    first, last = groups[group]
                    if first < last:
                        far_start(step, first, last)
                else:
                    half_far_start(group - len(groups), step)

    def backward_bunch(step, carry):
        for place in range(bunch):
            head_backward(bunch * step + place)
        for place in range(bunches):
            if place in PLAN:

                @pl.when(step == place)
                def _(place=place):
                    relay(place)

        @pl.when(step == bunches // 2 - 1)
        def _():
            half_grad(0)
            half_pair_start(0)

        return carry

    lax.fori_loop(0, bunches, backward_bunch, 0)
    half_grad(1)
    half_pair_start(1)
    relay(BEFORE_LAST)
    d_moved = d_hidden_s[...].astype(F32) + norm_back(
        moved_s[...].astype(F32), mm(w_qkv[...], d_packed_s[...])
    )
    fill(3, mm_t(land_sel[...], d_moved.astype(BF16)))
    send_all(3)
    relay(AFTER_LAST)

    land_all(2)
    out_feats[...] = mm(unpack_sel[...], arrived(2)).astype(BF16)

    relay(AT_END)

    @pl.when(level >= late)
    def _():
        weight_grads[...] = part_sum(stages, level)

    land_all(3)
    grad_feats[...] = mm(unpack_sel[...], arrived(3)).astype(BF16)

    @pl.when(level < late)
    def _():
        for half in range(2):
            flat[flat_half(level, side, half), :] = half_sum(half, stages, level)
        for col in range(cols_qkv):
            at = (2 * level + side) * share + (col % 2) * half_share + (col // 2) * slab
            weight_grads[pl.ds(col, slab, stride=cols_qkv), :] = flat[
                pl.ds(pl.multiple_of(at, 8), slab), :
            ]

    def pair_drain(step, carry):
        pair_copy(step).wait_send()
        return carry

    lax.fori_loop(late, outer, pair_drain, 0)

    def far_drain(stage):
        def wait(place, carry):
            part = part_of(stage, place)

            @pl.when(part >= late)
            def _():
                far_copy(stage, part).wait_send()

            @pl.when(part < late)
            def _():
                for half in range(2):
                    half_far_copy(half, stage, part).wait_send()

            return carry

        lax.fori_loop(0, outer // 2 ** (stage + 1), wait, 0)

    for stage in range(stages):
        far_drain(stage)

    def half_drain(step, carry):
        for half in range(2):
            half_pair_copy(half, step).wait_send()
        return carry

    lax.fori_loop(0, late, half_drain, 0)
    for which in range(4):
        drain(which)


def hand_over(*refs):
    count = len(refs) // 2
    sems = refs[-1]
    copies = [
        pltpu.make_async_copy(refs[place], refs[count + place], sems.at[place])
        for place in range(count)
    ]
    for copy in copies:
        copy.start()
    for copy in copies:
        copy.wait()


def body(feats, cotangent, w_qkv, w_out, w_up, w_down, hilbert_src, z_dest, valid_count):
    rows, chans = feats.shape
    hid = w_up.shape[1]
    shards = lax.axis_size("seq")
    slots = 2 * rows // shards
    outer = shards // 2
    packed = w_qkv.shape[1]
    flat_rows = (chans * packed + chans * chans + 2 * chans * hid) // LANES
    share = flat_rows // shards
    vmem = pl.BlockSpec(memory_space=pltpu.VMEM)
    dma = pltpu.SemaphoreType.DMA
    out_feats, grad_feats, weight_grads = pl.pallas_call(
        functools.partial(kernel, shards, slots),
        out_shape=(
            jax.ShapeDtypeStruct((rows, chans), BF16),
            jax.ShapeDtypeStruct((rows, chans), BF16),
            jax.ShapeDtypeStruct((share, LANES), F32),
        ),
        in_specs=[pl.BlockSpec(memory_space=pltpu.HBM)] * 9,
        out_specs=(vmem, vmem, vmem),
        scratch_shapes=[
            pltpu.VMEM((4, shards, slots, chans), BF16),
            pltpu.VMEM((4, shards, slots, chans), BF16),
            pltpu.VMEM((shards * slots, rows), BF16),
            pltpu.VMEM((rows, shards * slots), BF16),
            pltpu.VMEM((shards * slots, rows), BF16),
            pltpu.VMEM((packed, chans), BF16),
            pltpu.VMEM((chans, chans), BF16),
            pltpu.VMEM((hid, chans), BF16),
            pltpu.VMEM((chans, hid), BF16),
            pltpu.VMEM((chans, rows), BF16),
            pltpu.VMEM((chans, rows), BF16),
            pltpu.VMEM((packed, rows), BF16),
            pltpu.VMEM((chans, rows), BF16),
            pltpu.VMEM((chans, rows), BF16),
            pltpu.VMEM((chans, rows), BF16),
            pltpu.VMEM((hid, rows), BF16),
            pltpu.VMEM((hid, rows), F32),
            pltpu.VMEM((HEADS, rows, rows), BF16),
            pltpu.VMEM((HEADS, 1, rows), F32),
            pltpu.VMEM((chans, rows), BF16),
            pltpu.VMEM((chans, rows), BF16),
            pltpu.VMEM((packed, rows), BF16),
            pltpu.VMEM((flat_rows, LANES), F32),
            pltpu.VMEM((outer, share, LANES), BF16),
            pltpu.VMEM((outer, share, LANES), BF16),
            pltpu.VMEM((outer, share, LANES), BF16),
            pltpu.VMEM((outer, share, LANES), BF16),
            dma((4, shards)),
            dma((4, shards)),
            dma((outer,)),
            dma((outer,)),
            dma((outer,)),
            dma((outer,)),
            dma((2, outer)),
            dma((2, outer)),
            dma((2, outer)),
            dma((2, outer)),
            pltpu.VMEM((rows, chans), BF16),
            pltpu.VMEM((rows, chans), BF16),
            pltpu.VMEM((chans, packed), BF16),
            pltpu.VMEM((chans, chans), BF16),
            pltpu.VMEM((chans, hid), BF16),
            pltpu.VMEM((hid, chans), BF16),
            pltpu.VMEM((1, rows), jnp.int32),
            pltpu.VMEM((1, rows), jnp.int32),
            pltpu.SMEM((1,), jnp.int32),
            dma((9,)),
        ],
        compiler_params=pltpu.CompilerParams(
            collective_id=0, has_side_effects=True, vmem_limit_bytes=60 * 1024 * 1024
        ),
        name="block_step",
    )(
        feats,
        cotangent,
        w_qkv,
        w_out,
        w_up,
        w_down,
        hilbert_src.reshape(1, rows),
        z_dest.reshape(1, rows),
        valid_count,
    )
    results = (out_feats, grad_feats, weight_grads)
    far = vmem
    out_feats, grad_feats, weight_grads = pl.pallas_call(
        hand_over,
        out_shape=tuple(jax.ShapeDtypeStruct(array.shape, array.dtype) for array in results),
        in_specs=[far] * len(results),
        out_specs=(far,) * len(results),
        scratch_shapes=[dma((len(results),))],
        name="hand_over",
    )(*results)
    return out_feats, grad_feats, weight_grads.reshape(-1)


def solution(mesh):
    in_specs = (
        P(("dp", "seq"), None),
        P(("dp", "seq"), None),
        P(),
        P(),
        P(),
        P(),
        P(("dp", "seq")),
        P(("dp", "seq")),
        P(("dp", "seq")),
    )
    out_specs = (P(("dp", "seq"), None), P(("dp", "seq"), None), P(("dp", "seq")))
    return jax.shard_map(body, mesh=mesh, in_specs=in_specs, out_specs=out_specs, check_vma=False)
```

```python
import functools
import math

import jax
import jax.numpy as jnp
from jax import lax
from jax.experimental import pallas as pl
from jax.experimental.pallas import tpu as pltpu
from jax.sharding import PartitionSpec as P

HEADS = 16
F32 = jnp.float32
BF16 = jnp.bfloat16
LANES = 128
BUNCH = 4
BEFORE_LAST = 8
AFTER_LAST = 9
AT_END = 10
PLAN = {1: ((0, 0),), 3: ((1, 0),), 9: ((0, 1), (0, 2), (0, 3), (0, 4)), 10: ((1, 1), (1, 2), (1, 3), (1, 4))}
MESH = pl.DeviceIdType.MESH


def mm(left, right):
    return lax.dot_general(left, right, (((1,), (0,)), ((), ())), preferred_element_type=F32)


def mm_t(left, right):
    return lax.dot_general(left, right, (((1,), (1,)), ((), ())), preferred_element_type=F32)


def norm_parts(floats):
    center = jnp.mean(floats, axis=0, keepdims=True)
    gap = floats - center
    spread = jnp.mean(gap * gap, axis=0, keepdims=True)
    inverse = lax.rsqrt(spread + 1e-05)
    return gap * inverse, inverse


def norm_back(floats, upstream):
    normal, inverse = norm_parts(floats)
    first = jnp.mean(upstream, axis=0, keepdims=True)
    second = jnp.mean(upstream * normal, axis=0, keepdims=True)
    return inverse * (upstream - first - normal * second)


def column_of(row):
    return jnp.transpose(jnp.broadcast_to(row, (LANES, row.shape[1])))[:, :1]


def one_hot(rows, cols, match):
    return jnp.where(match, jnp.ones((rows, cols), F32), jnp.zeros((rows, cols), F32)).astype(BF16)


def kernel(
    shards,
    slots,
    feats_far,
    cotangent_far,
    w_qkv_far,
    w_out_far,
    w_up_far,
    w_down_far,
    hilbert_src_far,
    z_dest_far,
    valid_count_far,
    out_feats,
    grad_feats,
    weight_grads,
    outbox,
    inbox,
    pack_sel,
    unpack_sel,
    land_sel,
    w_qkv_t,
    w_out_t,
    w_up_t,
    w_down_t,
    moved_s,
    normed_s,
    packed_s,
    mixed_s,
    hidden_s,
    normed_two_s,
    act_s,
    slope_s,
    weights_s,
    inverse_s,
    d_mixed_s,
    d_hidden_s,
    d_packed_s,
    flat,
    pair_out,
    pair_in,
    far_out,
    far_in,
    send_sem,
    recv_sem,
    pair_send,
    pair_recv,
    far_send,
    far_recv,
    half_pair_send,
    half_pair_recv,
    half_far_send,
    half_far_recv,
    feats,
    cotangent,
    w_qkv,
    w_out,
    w_up,
    w_down,
    hilbert_src,
    z_dest,
    valid_count,
    load_sem,
):
    me = lax.axis_index("seq")
    rows, chans = feats.shape
    heads = HEADS
    depth = chans // heads
    hid = w_up.shape[1]
    outer = shards // 2
    share = weight_grads.shape[0]
    side = lax.rem(me, 2)
    mate = me + 1 - 2 * side
    level = lax.div(me, 2)

    barrier = pltpu.get_barrier_semaphore()

    def greet(step, carry):
        peer = lax.rem(me + step, shards)
        pl.semaphore_signal(barrier, inc=1, device_id={"seq": peer}, device_id_type=MESH)
        return carry

    lax.fori_loop(1, shards, greet, 0)

    fetches = {}
    for place, (source, here) in enumerate(
        (
            (z_dest_far, z_dest),
            (feats_far, feats),
            (cotangent_far, cotangent),
            (hilbert_src_far, hilbert_src),
            (w_qkv_far, w_qkv),
            (valid_count_far, valid_count),
            (w_out_far, w_out),
            (w_up_far, w_up),
            (w_down_far, w_down),
        )
    ):
        fetches[place] = pltpu.make_async_copy(source, here, load_sem.at[place])
        fetches[place].start()

    def box(which, home, peer, device):
        return pltpu.make_async_remote_copy(
            src_ref=outbox.at[which, peer],
            dst_ref=inbox.at[which, home],
            send_sem=send_sem.at[which, peer],
            recv_sem=recv_sem.at[which, home],
            device_id={"seq": device},
            device_id_type=MESH,
        )

    def send_one(which, jump):
        peer = lax.rem(me + jump, shards)
        box(which, me, peer, peer).start()

    def send_all(which):
        def start(step, carry):
            send_one(which, outer + (1 - 2 * lax.rem(step, 2)) * (step // 2))
            return carry

        lax.fori_loop(1, shards, start, 0)

    def send_odd(which, odd):
        def start(step, carry):
            @pl.when(lax.rem(outer + (1 - 2 * lax.rem(step, 2)) * (step // 2), 2) == odd)
            def _():
                send_one(which, outer + (1 - 2 * lax.rem(step, 2)) * (step // 2))

            return carry

        lax.fori_loop(1, shards, start, 0)

    def land_all(which):
        def wait(step, carry):
            peer = lax.rem(me + step, shards)
            box(which, peer, peer, peer).wait_recv()
            return carry

        lax.fori_loop(1, shards, wait, 0)

    def drain(which):
        def wait(step, carry):
            peer = lax.rem(me + step, shards)
            box(which, me, peer, peer).wait_send()
            return carry

        lax.fori_loop(1, shards, wait, 0)

    def fill(which, values):
        outbox[which] = values.reshape(shards, slots, chans).astype(BF16)
        inbox[which, me] = outbox[which, me]

    def arrived(which):
        block = inbox[which]
        if slots % 16:
            return block.astype(F32).reshape(shards * slots, chans).astype(BF16)
        return block.reshape(shards * slots, chans)

    fetches[0].wait()
    z_row = z_dest[...]
    target = lax.div(z_row, jnp.full_like(z_row, rows))
    low = target * rows
    z_col = column_of(z_row)
    before = jnp.logical_and(z_col < z_row, z_col >= low)
    rank = jnp.sum(jnp.where(before, 1.0, 0.0).astype(F32), axis=0, keepdims=True)
    send_row = target * slots + rank.astype(jnp.int32)
    slot_ids = lax.broadcasted_iota(jnp.int32, (shards * slots, rows), 0)
    pack_sel[...] = one_hot(shards * slots, rows, slot_ids == send_row)
    fetches[1].wait()
    fill(0, mm(pack_sel[...], feats[...]))
    pl.semaphore_wait(barrier, shards - 1)
    send_all(0)
    fetches[2].wait()
    fill(1, mm(pack_sel[...], cotangent[...]))

    fetches[3].wait()
    h_row = hilbert_src[...]
    source = lax.div(h_row, jnp.full_like(h_row, rows))
    source_col = column_of(source)
    first_ids = lax.broadcasted_iota(jnp.int32, (rows, rows), 0)
    second_ids = lax.broadcasted_iota(jnp.int32, (rows, rows), 1)
    before = jnp.logical_and(source_col == source, first_ids < second_ids)
    rank = jnp.sum(jnp.where(before, 1.0, 0.0).astype(F32), axis=0, keepdims=True)
    land_row = source * slots + rank.astype(jnp.int32)
    land_sel[...] = one_hot(shards * slots, rows, slot_ids == land_row)
    lane_ids = lax.broadcasted_iota(jnp.int32, (rows, shards * slots), 1)
    unpack_sel[...] = one_hot(rows, shards * slots, lane_ids == column_of(send_row))

    for place in range(4, 9):
        fetches[place].wait()
    w_qkv_t[...] = jnp.transpose(w_qkv[...])
    w_out_t[...] = jnp.transpose(w_out[...])
    w_up_t[...] = jnp.transpose(w_up[...])
    w_down_t[...] = jnp.transpose(w_down[...])

    point_ids = lax.broadcasted_iota(jnp.int32, (1, rows), 1)
    kept = point_ids < valid_count[0]
    keep = jnp.where(kept, 1.0, 0.0).astype(F32)
    bias = jnp.where(kept, 0.0, -1000000000.0).astype(F32)
    row_ids = lax.broadcasted_iota(jnp.int32, (depth, rows), 0)
    bias_rows = jnp.where(row_ids == 0, jnp.broadcast_to(bias, (depth, rows)), 0.0).astype(BF16)
    one_rows = jnp.where(row_ids == 0, 1.0, 0.0).astype(BF16)
    two_rows = jnp.where(row_ids < 2, 1.0, 0.0).astype(BF16)

    land_all(0)
    send_all(1)
    moved = mm(jnp.transpose(arrived(0)), land_sel[...])
    moved_s[...] = moved.astype(BF16)
    normal, _ = norm_parts(moved)
    normed_s[...] = normal.astype(BF16)
    packed_s[...] = mm(w_qkv_t[...], normed_s[...]).astype(BF16)
    factor = depth ** (-0.5)

    def head_forward(head):
        at = pl.multiple_of(head * depth, depth)
        query = packed_s[pl.ds(at, depth), :] * jnp.asarray(factor, BF16)
        keys = packed_s[pl.ds(chans + at, depth), :]
        values = packed_s[pl.ds(2 * chans + at, depth), :]
        query_more = jnp.concatenate([query, one_rows], axis=0)
        keys_more = jnp.transpose(jnp.concatenate([keys, bias_rows], axis=0))
        values_more = jnp.concatenate([values, one_rows], axis=0)
        scores = mm(keys_more, query_more)
        highest = jnp.max(scores, axis=0, keepdims=True)
        weights = jnp.exp(scores - highest).astype(BF16)
        weights_s[head] = weights
        total = mm(values_more, weights)
        inverse = 1.0 / total[depth : depth + 1]
        inverse_s[head] = inverse
        mixed_s[pl.ds(at, depth), :] = (total[:depth] * inverse).astype(BF16)

    bunch = math.gcd(heads, BUNCH)

    def forward_bunch(step, carry):
        for place in range(bunch):
            head_forward(bunch * step + place)
        return carry

    lax.fori_loop(0, heads // bunch, forward_bunch, 0)

    hidden = moved_s[...].astype(F32) + keep * mm(w_out_t[...], mixed_s[...])
    hidden_s[...] = hidden.astype(BF16)
    normal, _ = norm_parts(hidden_s[...].astype(F32))
    normed_two_s[...] = normal.astype(BF16)
    inner = math.sqrt(2.0 / math.pi)
    piece = math.gcd(hid, LANES)

    def up_piece(step, carry):
        at = pl.multiple_of(step * piece, piece)
        pre = mm(w_up_t[pl.ds(at, piece), :], normed_two_s[...])
        curve = jnp.tanh(inner * (pre + 0.044715 * pre * pre * pre))
        act_s[pl.ds(at, piece), :] = (pre * (0.5 * (1.0 + curve))).astype(BF16)
        slope_s[pl.ds(at, piece), :] = pre
        return carry

    lax.fori_loop(0, hid // piece, up_piece, 0)
    at_out = chans * 3 * chans // LANES
    at_up = at_out + chans * chans // LANES
    at_down = at_up + chans * hid // LANES
    cols_qkv = 3 * chans // LANES
    late = at_out // (2 * share)
    ready = -(-at_down // (2 * share))
    early = outer - late
    half_share = share // 2
    stages = outer.bit_length() - 1
    middle = min(2 * late, ready)
    slab = share // cols_qkv

    def spread_flat(start, grad):
        stride = grad.shape[1] // LANES
        for col in range(stride):
            flat[pl.ds(start + col, grad.shape[0], stride=stride), :] = grad[
                :, col * LANES : (col + 1) * LANES
            ]

    def pair_copy(step):
        return pltpu.make_async_remote_copy(
            src_ref=pair_out.at[step],
            dst_ref=pair_in.at[step],
            send_sem=pair_send.at[step],
            recv_sem=pair_recv.at[step],
            device_id={"seq": mate},
            device_id_type=MESH,
        )

    def keep_bit(stage):
        return lax.rem(lax.div(level, 2**stage), 2)

    def partner(stage):
        return me + 2 ** (stage + 1) * (1 - 2 * keep_bit(stage))

    def part_of(stage, place):
        low = lax.rem(level, 2**stage)
        return low + 2**stage * (1 - keep_bit(stage)) + 2 ** (stage + 1) * place

    def far_slot(stage, part):
        return outer - outer // 2**stage + lax.div(part, 2 ** (stage + 1))

    def far_copy(stage, part):
        slot = far_slot(stage, part)
        return pltpu.make_async_remote_copy(
            src_ref=far_out.at[part],
            dst_ref=far_in.at[slot],
            send_sem=far_send.at[part],
            recv_sem=far_recv.at[slot],
            device_id={"seq": partner(stage)},
            device_id_type=MESH,
        )

    def half_rows(half):
        return pl.ds(half * half_share, half_share)

    def half_pair_copy(half, step):
        return pltpu.make_async_remote_copy(
            src_ref=pair_out.at[step, half_rows(half)],
            dst_ref=pair_in.at[step, half_rows(half)],
            send_sem=half_pair_send.at[half, step],
            recv_sem=half_pair_recv.at[half, step],
            device_id={"seq": mate},
            device_id_type=MESH,
        )

    def half_far_copy(half, stage, part):
        slot = far_slot(stage, part)
        return pltpu.make_async_remote_copy(
            src_ref=far_out.at[part, half_rows(half)],
            dst_ref=far_in.at[slot, half_rows(half)],
            send_sem=half_far_send.at[half, part],
            recv_sem=half_far_recv.at[half, slot],
            device_id={"seq": partner(stage)},
            device_id_type=MESH,
        )

    def flat_rows(step, which):
        return pl.ds(pl.multiple_of((2 * step + which) * share, 16), share)

    def flat_half(step, which, half):
        at = (2 * step + which) * share + half * half_share
        return pl.ds(pl.multiple_of(at, 8), half_share)

    def pair_start(step, carry):
        pair_out[step] = flat[flat_rows(step, 1 - side), :].astype(BF16)
        pair_copy(step).start()
        return carry

    def part_sum(stage, part):
        pair_copy(part).wait_recv()
        total = flat[flat_rows(part, side), :] + pair_in[part].astype(F32)
        for before in range(stage):
            far_copy(before, part).wait_recv()
            total = total + far_in[far_slot(before, part)].astype(F32)
        return total

    def far_start(stage, first, last):
        def start(place, carry):
            part = part_of(stage, place)

            @pl.when(jnp.logical_and(part >= first, part < last))
            def _():
                far_out[part] = part_sum(stage, part).astype(BF16)
                far_copy(stage, part).start()

            return carry

        lax.fori_loop(0, outer // 2 ** (stage + 1), start, 0)

    def half_grad(half):
        for col in range(half, cols_qkv, 2):
            grad = mm_t(normed_s[...], d_packed_s[col * LANES : (col + 1) * LANES, :])
            for shard in range(2 * late):
                at = shard * share + half * half_share + (col // 2) * slab
                flat[at : at + slab, :] = grad[shard * slab : (shard + 1) * slab]

    def half_pair_start(half):
        def start(step, carry):
            pair_out[step, half_rows(half)] = flat[flat_half(step, 1 - side, half), :].astype(BF16)
            half_pair_copy(half, step).start()
            return carry

        lax.fori_loop(0, late, start, 0)

    def half_sum(half, stage, part):
        half_pair_copy(half, part).wait_recv()
        total = flat[flat_half(part, side, half), :]
        total = total + pair_in[part, half_rows(half)].astype(F32)
        for before in range(stage):
            half_far_copy(half, before, part).wait_recv()
            total = total + far_in[far_slot(before, part), half_rows(half)].astype(F32)
        return total

    def half_far_start(half, stage):
        def start(place, carry):
            part = part_of(stage, place)

            @pl.when(part < late)
            def _():
                far_out[part, half_rows(half)] = half_sum(half, stage, part).astype(BF16)
                half_far_copy(half, stage, part).start()

            return carry

        lax.fori_loop(0, outer // 2 ** (stage + 1), start, 0)

    land_all(1)
    upstream = mm(jnp.transpose(arrived(1)), land_sel[...])
    branch = (keep * upstream).astype(BF16)
    spread_flat(at_down, mm_t(act_s[...], branch))
    lax.fori_loop(ready, outer, pair_start, 0)
    block = hidden_s[...].astype(F32) + keep * mm(w_down_t[...], act_s[...])
    fill(2, mm_t(land_sel[...], block.astype(BF16)))
    send_all(2)

    def down_piece(step, carry):
        at = pl.multiple_of(step * piece, piece)
        d_act = mm(w_down[pl.ds(at, piece), :], branch)
        pre = slope_s[pl.ds(at, piece), :]
        square = pre * pre
        curve = jnp.tanh(inner * (pre + 0.044715 * square * pre))
        bend = 0.5 * (1.0 - curve * curve) * (inner * (1.0 + 3.0 * 0.044715 * square))
        slope = 0.5 * (1.0 + curve) + pre * bend
        act_s[pl.ds(at, piece), :] = (d_act * slope).astype(BF16)
        return carry

    lax.fori_loop(0, hid // piece, down_piece, 0)
    spread_flat(at_up, mm_t(normed_two_s[...], act_s[...]))
    d_hidden = upstream + norm_back(hidden_s[...].astype(F32), mm(w_up[...], act_s[...]))
    d_hidden_s[...] = d_hidden.astype(BF16)
    branch_one = (keep * d_hidden_s[...].astype(F32)).astype(BF16)
    spread_flat(at_out, mm_t(mixed_s[...], branch_one))
    d_mixed_s[...] = mm(w_out[...], branch_one).astype(BF16)

    def head_backward(head):
        at = pl.multiple_of(head * depth, depth)
        query = packed_s[pl.ds(at, depth), :] * jnp.asarray(factor, BF16)
        keys = packed_s[pl.ds(chans + at, depth), :]
        values = packed_s[pl.ds(2 * chans + at, depth), :]
        values_more = jnp.transpose(jnp.concatenate([values, two_rows], axis=0))
        scaled = (d_mixed_s[pl.ds(at, depth), :].astype(F32) * inverse_s[head]).astype(BF16)
        mixed = mixed_s[pl.ds(at, depth), :].astype(F32)
        delta = -jnp.sum(scaled.astype(F32) * mixed, axis=0, keepdims=True)
        coarse = delta.astype(BF16).astype(F32)
        fine = delta - coarse
        tail = jnp.where(
            row_ids == 0,
            jnp.broadcast_to(coarse, (depth, rows)),
            jnp.where(row_ids == 1, jnp.broadcast_to(fine, (depth, rows)), 0.0),
        ).astype(BF16)
        scaled_more = jnp.concatenate([scaled, tail], axis=0)
        weights = weights_s[head]
        gap = mm(values_more, scaled_more).astype(BF16)
        d_scores = weights * gap
        d_query = mm(keys, d_scores) * factor
        d_packed_s[pl.ds(at, depth), :] = d_query.astype(BF16)
        d_packed_s[pl.ds(chans + at, depth), :] = mm_t(query, d_scores).astype(BF16)
        d_packed_s[pl.ds(2 * chans + at, depth), :] = mm_t(scaled, weights).astype(BF16)

    lax.fori_loop(late, ready, pair_start, 0)

    bunches = heads // bunch

    groups = ((ready, outer), (middle, ready), (late, middle))

    def relay(place):
        for stage, group in PLAN.get(place, ()):
            for step in (stage,) if stage == 0 else range(stage, stages):
                if group < len(groups):
                    first, last = groups[group]
                    if first < last:
                        far_start(step, first, last)
                else:
                    half_far_start(group - len(groups), step)

    def backward_bunch(step, carry):
        for place in range(bunch):
            head_backward(bunch * step + place)
        for place in range(bunches):
            if place in PLAN:

                @pl.when(step == place)
                def _(place=place):
                    relay(place)

        @pl.when(step == bunches // 2 - 1)
        def _():
            half_grad(0)
            half_pair_start(0)

        return carry

    lax.fori_loop(0, bunches, backward_bunch, 0)
    half_grad(1)
    half_pair_start(1)
    relay(BEFORE_LAST)
    d_moved = d_hidden_s[...].astype(F32) + norm_back(
        moved_s[...].astype(F32), mm(w_qkv[...], d_packed_s[...])
    )
    fill(3, mm_t(land_sel[...], d_moved.astype(BF16)))
    send_all(3)
    relay(AFTER_LAST)

    land_all(2)
    out_feats[...] = mm(unpack_sel[...], arrived(2)).astype(BF16)

    relay(AT_END)

    @pl.when(level >= late)
    def _():
        weight_grads[...] = part_sum(stages, level)

    land_all(3)
    grad_feats[...] = mm(unpack_sel[...], arrived(3)).astype(BF16)

    @pl.when(level < late)
    def _():
        for half in range(2):
            flat[flat_half(level, side, half), :] = half_sum(half, stages, level)
        for col in range(cols_qkv):
            at = (2 * level + side) * share + (col % 2) * half_share + (col // 2) * slab
            weight_grads[pl.ds(col, slab, stride=cols_qkv), :] = flat[
                pl.ds(pl.multiple_of(at, 8), slab), :
            ]

    def pair_drain(step, carry):
        pair_copy(step).wait_send()
        return carry

    lax.fori_loop(late, outer, pair_drain, 0)

    def far_drain(stage):
        def wait(place, carry):
            part = part_of(stage, place)

            @pl.when(part >= late)
            def _():
                far_copy(stage, part).wait_send()

            @pl.when(part < late)
            def _():
                for half in range(2):
                    half_far_copy(half, stage, part).wait_send()

            return carry

        lax.fori_loop(0, outer // 2 ** (stage + 1), wait, 0)

    for stage in range(stages):
        far_drain(stage)

    def half_drain(step, carry):
        for half in range(2):
            half_pair_copy(half, step).wait_send()
        return carry

    lax.fori_loop(0, late, half_drain, 0)
    for which in range(4):
        drain(which)


def hand_over(*refs):
    count = (len(refs) - 2) // 3
    sources, targets, helds = (refs[count * place : count * (place + 1)] for place in range(3))
    load_sem, store_sem = refs[3 * count :]
    loads = [
        pltpu.make_async_copy(sources[place], helds[place], load_sem.at[place])
        for place in range(count)
    ]
    stores = [
        pltpu.make_async_copy(helds[place], targets[place], store_sem.at[place])
        for place in range(count)
    ]
    for load in loads:
        load.start()
    for load, store in zip(loads, stores):
        load.wait()
        store.start()
    for store in stores:
        store.wait()


def body(feats, cotangent, w_qkv, w_out, w_up, w_down, hilbert_src, z_dest, valid_count):
    rows, chans = feats.shape
    hid = w_up.shape[1]
    shards = lax.axis_size("seq")
    slots = 2 * rows // shards
    outer = shards // 2
    packed = w_qkv.shape[1]
    flat_rows = (chans * packed + chans * chans + 2 * chans * hid) // LANES
    share = flat_rows // shards
    vmem = pl.BlockSpec(memory_space=pltpu.VMEM)
    dma = pltpu.SemaphoreType.DMA
    out_feats, grad_feats, weight_grads = pl.pallas_call(
        functools.partial(kernel, shards, slots),
        out_shape=(
            jax.ShapeDtypeStruct((rows, chans), BF16),
            jax.ShapeDtypeStruct((rows, chans), BF16),
            jax.ShapeDtypeStruct((share, LANES), F32),
        ),
        in_specs=[pl.BlockSpec(memory_space=pltpu.HBM)] * 9,
        out_specs=(vmem, vmem, vmem),
        scratch_shapes=[
            pltpu.VMEM((4, shards, slots, chans), BF16),
            pltpu.VMEM((4, shards, slots, chans), BF16),
            pltpu.VMEM((shards * slots, rows), BF16),
            pltpu.VMEM((rows, shards * slots), BF16),
            pltpu.VMEM((shards * slots, rows), BF16),
            pltpu.VMEM((packed, chans), BF16),
            pltpu.VMEM((chans, chans), BF16),
            pltpu.VMEM((hid, chans), BF16),
            pltpu.VMEM((chans, hid), BF16),
            pltpu.VMEM((chans, rows), BF16),
            pltpu.VMEM((chans, rows), BF16),
            pltpu.VMEM((packed, rows), BF16),
            pltpu.VMEM((chans, rows), BF16),
            pltpu.VMEM((chans, rows), BF16),
            pltpu.VMEM((chans, rows), BF16),
            pltpu.VMEM((hid, rows), BF16),
            pltpu.VMEM((hid, rows), F32),
            pltpu.VMEM((HEADS, rows, rows), BF16),
            pltpu.VMEM((HEADS, 1, rows), F32),
            pltpu.VMEM((chans, rows), BF16),
            pltpu.VMEM((chans, rows), BF16),
            pltpu.VMEM((packed, rows), BF16),
            pltpu.VMEM((flat_rows, LANES), F32),
            pltpu.VMEM((outer, share, LANES), BF16),
            pltpu.VMEM((outer, share, LANES), BF16),
            pltpu.VMEM((outer, share, LANES), BF16),
            pltpu.VMEM((outer, share, LANES), BF16),
            dma((4, shards)),
            dma((4, shards)),
            dma((outer,)),
            dma((outer,)),
            dma((outer,)),
            dma((outer,)),
            dma((2, outer)),
            dma((2, outer)),
            dma((2, outer)),
            dma((2, outer)),
            pltpu.VMEM((rows, chans), BF16),
            pltpu.VMEM((rows, chans), BF16),
            pltpu.VMEM((chans, packed), BF16),
            pltpu.VMEM((chans, chans), BF16),
            pltpu.VMEM((chans, hid), BF16),
            pltpu.VMEM((hid, chans), BF16),
            pltpu.VMEM((1, rows), jnp.int32),
            pltpu.VMEM((1, rows), jnp.int32),
            pltpu.SMEM((1,), jnp.int32),
            dma((9,)),
        ],
        compiler_params=pltpu.CompilerParams(
            collective_id=0, has_side_effects=True, vmem_limit_bytes=60 * 1024 * 1024
        ),
        name="block_step",
    )(
        feats,
        cotangent,
        w_qkv,
        w_out,
        w_up,
        w_down,
        hilbert_src.reshape(1, rows),
        z_dest.reshape(1, rows),
        valid_count,
    )
    results = (out_feats, grad_feats, weight_grads)
    far = pl.BlockSpec(memory_space=pltpu.HBM)
    out_feats, grad_feats, weight_grads = pl.pallas_call(
        hand_over,
        out_shape=tuple(jax.ShapeDtypeStruct(array.shape, array.dtype) for array in results),
        in_specs=[far] * len(results),
        out_specs=(far,) * len(results),
        scratch_shapes=[pltpu.VMEM(array.shape, array.dtype) for array in results]
        + [dma((len(results),)), dma((len(results),))],
        name="hand_over",
    )(*results)
    return out_feats, grad_feats, weight_grads.reshape(-1)


def solution(mesh):
    in_specs = (
        P(("dp", "seq"), None),
        P(("dp", "seq"), None),
        P(),
        P(),
        P(),
        P(),
        P(("dp", "seq")),
        P(("dp", "seq")),
        P(("dp", "seq")),
    )
    out_specs = (P(("dp", "seq"), None), P(("dp", "seq"), None), P(("dp", "seq")))
    return jax.shard_map(body, mesh=mesh, in_specs=in_specs, out_specs=out_specs, check_vma=False)
```

```python
import functools
import math

import jax
import jax.numpy as jnp
from jax import lax
from jax.experimental import pallas as pl
from jax.experimental.pallas import tpu as pltpu
from jax.sharding import PartitionSpec as P

HEADS = 16
F32 = jnp.float32
BF16 = jnp.bfloat16
LANES = 128
BUNCH = 4
BEFORE_LAST = 8
AFTER_LAST = 9
AT_END = 10
PLAN = {1: ((0, 0),), 3: ((1, 0),), 9: ((0, 1), (0, 2), (0, 3), (0, 4)), 10: ((1, 1), (1, 2), (1, 3), (1, 4))}
MESH = pl.DeviceIdType.MESH


def mm(left, right):
    return lax.dot_general(left, right, (((1,), (0,)), ((), ())), preferred_element_type=F32)


def mm_t(left, right):
    return lax.dot_general(left, right, (((1,), (1,)), ((), ())), preferred_element_type=F32)


def norm_parts(floats):
    center = jnp.mean(floats, axis=0, keepdims=True)
    gap = floats - center
    spread = jnp.mean(gap * gap, axis=0, keepdims=True)
    inverse = lax.rsqrt(spread + 1e-05)
    return gap * inverse, inverse


def norm_back(floats, upstream):
    normal, inverse = norm_parts(floats)
    first = jnp.mean(upstream, axis=0, keepdims=True)
    second = jnp.mean(upstream * normal, axis=0, keepdims=True)
    return inverse * (upstream - first - normal * second)


def column_of(row):
    return jnp.transpose(jnp.broadcast_to(row, (LANES, row.shape[1])))[:, :1]


def one_hot(rows, cols, match):
    return jnp.where(match, jnp.ones((rows, cols), F32), jnp.zeros((rows, cols), F32)).astype(BF16)


def kernel(
    shards,
    slots,
    feats_far,
    cotangent_far,
    w_qkv_far,
    w_out_far,
    w_up_far,
    w_down_far,
    hilbert_src_far,
    z_dest_far,
    valid_count_far,
    out_feats,
    grad_feats,
    weight_grads,
    outbox,
    inbox,
    pack_sel,
    unpack_sel,
    land_sel,
    w_qkv_t,
    w_out_t,
    w_up_t,
    w_down_t,
    moved_s,
    normed_s,
    packed_s,
    mixed_s,
    hidden_s,
    normed_two_s,
    act_s,
    slope_s,
    weights_s,
    inverse_s,
    d_mixed_s,
    d_hidden_s,
    d_packed_s,
    flat,
    pair_out,
    pair_in,
    far_out,
    far_in,
    send_sem,
    recv_sem,
    pair_send,
    pair_recv,
    far_send,
    far_recv,
    half_pair_send,
    half_pair_recv,
    half_far_send,
    half_far_recv,
    feats,
    cotangent,
    w_qkv,
    w_out,
    w_up,
    w_down,
    hilbert_src,
    z_dest,
    valid_count,
    load_sem,
):
    me = lax.axis_index("seq")
    rows, chans = feats.shape
    heads = HEADS
    depth = chans // heads
    hid = w_up.shape[1]
    outer = shards // 2
    share = weight_grads.shape[0]
    side = lax.rem(me, 2)
    mate = me + 1 - 2 * side
    level = lax.div(me, 2)

    barrier = pltpu.get_barrier_semaphore()

    def greet(step, carry):
        peer = lax.rem(me + step, shards)
        pl.semaphore_signal(barrier, inc=1, device_id={"seq": peer}, device_id_type=MESH)
        return carry

    lax.fori_loop(1, shards, greet, 0)

    fetches = {}
    for place, (source, here) in enumerate(
        (
            (z_dest_far, z_dest),
            (feats_far, feats),
            (cotangent_far, cotangent),
            (hilbert_src_far, hilbert_src),
            (w_qkv_far, w_qkv),
            (valid_count_far, valid_count),
            (w_out_far, w_out),
            (w_up_far, w_up),
            (w_down_far, w_down),
        )
    ):
        fetches[place] = pltpu.make_async_copy(source, here, load_sem.at[place])
        fetches[place].start()

    def box(which, home, peer, device):
        return pltpu.make_async_remote_copy(
            src_ref=outbox.at[which, peer],
            dst_ref=inbox.at[which, home],
            send_sem=send_sem.at[which, peer],
            recv_sem=recv_sem.at[which, home],
            device_id={"seq": device},
            device_id_type=MESH,
        )

    def send_one(which, jump):
        peer = lax.rem(me + jump, shards)
        box(which, me, peer, peer).start()

    def send_all(which):
        def start(step, carry):
            send_one(which, outer + (1 - 2 * lax.rem(step, 2)) * (step // 2))
            return carry

        lax.fori_loop(1, shards, start, 0)

    def send_odd(which, odd):
        def start(step, carry):
            @pl.when(lax.rem(outer + (1 - 2 * lax.rem(step, 2)) * (step // 2), 2) == odd)
            def _():
                send_one(which, outer + (1 - 2 * lax.rem(step, 2)) * (step // 2))

            return carry

        lax.fori_loop(1, shards, start, 0)

    def land_all(which):
        def wait(step, carry):
            peer = lax.rem(me + step, shards)
            box(which, peer, peer, peer).wait_recv()
            return carry

        lax.fori_loop(1, shards, wait, 0)

    def drain(which):
        def wait(step, carry):
            peer = lax.rem(me + step, shards)
            box(which, me, peer, peer).wait_send()
            return carry

        lax.fori_loop(1, shards, wait, 0)

    def fill(which, values):
        outbox[which] = values.reshape(shards, slots, chans).astype(BF16)
        inbox[which, me] = outbox[which, me]

    def arrived(which):
        block = inbox[which]
        if slots % 16:
            return block.astype(F32).reshape(shards * slots, chans).astype(BF16)
        return block.reshape(shards * slots, chans)

    fetches[0].wait()
    z_row = z_dest[...]
    target = lax.div(z_row, jnp.full_like(z_row, rows))
    low = target * rows
    z_col = column_of(z_row)
    before = jnp.logical_and(z_col < z_row, z_col >= low)
    rank = jnp.sum(jnp.where(before, 1.0, 0.0).astype(F32), axis=0, keepdims=True)
    send_row = target * slots + rank.astype(jnp.int32)
    slot_ids = lax.broadcasted_iota(jnp.int32, (shards * slots, rows), 0)
    pack_sel[...] = one_hot(shards * slots, rows, slot_ids == send_row)
    fetches[1].wait()
    fill(0, mm(pack_sel[...], feats[...]))
    pl.semaphore_wait(barrier, shards - 1)
    send_all(0)
    fetches[2].wait()
    fill(1, mm(pack_sel[...], cotangent[...]))

    fetches[3].wait()
    h_row = hilbert_src[...]
    source = lax.div(h_row, jnp.full_like(h_row, rows))
    source_col = column_of(source)
    first_ids = lax.broadcasted_iota(jnp.int32, (rows, rows), 0)
    second_ids = lax.broadcasted_iota(jnp.int32, (rows, rows), 1)
    before = jnp.logical_and(source_col == source, first_ids < second_ids)
    rank = jnp.sum(jnp.where(before, 1.0, 0.0).astype(F32), axis=0, keepdims=True)
    land_row = source * slots + rank.astype(jnp.int32)
    land_sel[...] = one_hot(shards * slots, rows, slot_ids == land_row)
    lane_ids = lax.broadcasted_iota(jnp.int32, (rows, shards * slots), 1)
    unpack_sel[...] = one_hot(rows, shards * slots, lane_ids == column_of(send_row))

    for place in range(4, 9):
        fetches[place].wait()
    w_qkv_t[...] = jnp.transpose(w_qkv[...])
    w_out_t[...] = jnp.transpose(w_out[...])
    w_up_t[...] = jnp.transpose(w_up[...])
    w_down_t[...] = jnp.transpose(w_down[...])

    point_ids = lax.broadcasted_iota(jnp.int32, (1, rows), 1)
    kept = point_ids < valid_count[0]
    keep = jnp.where(kept, 1.0, 0.0).astype(F32)
    bias = jnp.where(kept, 0.0, -1000000000.0).astype(F32)
    row_ids = lax.broadcasted_iota(jnp.int32, (depth, rows), 0)
    bias_rows = jnp.where(row_ids == 0, jnp.broadcast_to(bias, (depth, rows)), 0.0).astype(BF16)
    one_rows = jnp.where(row_ids == 0, 1.0, 0.0).astype(BF16)
    two_rows = jnp.where(row_ids < 2, 1.0, 0.0).astype(BF16)

    land_all(0)
    send_all(1)
    moved = mm(jnp.transpose(arrived(0)), land_sel[...])
    moved_s[...] = moved.astype(BF16)
    normal, _ = norm_parts(moved)
    normed_s[...] = normal.astype(BF16)
    packed_s[...] = mm(w_qkv_t[...], normed_s[...]).astype(BF16)
    factor = depth ** (-0.5)

    def head_forward(head):
        at = pl.multiple_of(head * depth, depth)
        query = packed_s[pl.ds(at, depth), :] * jnp.asarray(factor, BF16)
        keys = packed_s[pl.ds(chans + at, depth), :]
        values = packed_s[pl.ds(2 * chans + at, depth), :]
        query_more = jnp.concatenate([query, one_rows], axis=0)
        keys_more = jnp.transpose(jnp.concatenate([keys, bias_rows], axis=0))
        values_more = jnp.concatenate([values, one_rows], axis=0)
        scores = mm(keys_more, query_more)
        highest = jnp.max(scores, axis=0, keepdims=True)
        weights = jnp.exp(scores - highest).astype(BF16)
        weights_s[head] = weights
        total = mm(values_more, weights)
        inverse = 1.0 / total[depth : depth + 1]
        inverse_s[head] = inverse
        mixed_s[pl.ds(at, depth), :] = (total[:depth] * inverse).astype(BF16)

    bunch = math.gcd(heads, BUNCH)

    def forward_bunch(step, carry):
        for place in range(bunch):
            head_forward(bunch * step + place)
        return carry

    lax.fori_loop(0, heads // bunch, forward_bunch, 0)

    hidden = moved_s[...].astype(F32) + keep * mm(w_out_t[...], mixed_s[...])
    hidden_s[...] = hidden.astype(BF16)
    normal, _ = norm_parts(hidden_s[...].astype(F32))
    normed_two_s[...] = normal.astype(BF16)
    inner = math.sqrt(2.0 / math.pi)
    piece = math.gcd(hid, LANES)

    def up_piece(step, carry):
        at = pl.multiple_of(step * piece, piece)
        pre = mm(w_up_t[pl.ds(at, piece), :], normed_two_s[...])
        curve = jnp.tanh(inner * (pre + 0.044715 * pre * pre * pre))
        act_s[pl.ds(at, piece), :] = (pre * (0.5 * (1.0 + curve))).astype(BF16)
        slope_s[pl.ds(at, piece), :] = pre
        return carry

    lax.fori_loop(0, hid // piece, up_piece, 0)
    at_out = chans * 3 * chans // LANES
    at_up = at_out + chans * chans // LANES
    at_down = at_up + chans * hid // LANES
    cols_qkv = 3 * chans // LANES
    late = at_out // (2 * share)
    ready = -(-at_down // (2 * share))
    early = outer - late
    half_share = share // 2
    stages = outer.bit_length() - 1
    middle = min(2 * late, ready)
    slab = share // cols_qkv

    def spread_flat(start, grad):
        stride = grad.shape[1] // LANES
        for col in range(stride):
            flat[pl.ds(start + col, grad.shape[0], stride=stride), :] = grad[
                :, col * LANES : (col + 1) * LANES
            ]

    def pair_copy(step):
        return pltpu.make_async_remote_copy(
            src_ref=pair_out.at[step],
            dst_ref=pair_in.at[step],
            send_sem=pair_send.at[step],
            recv_sem=pair_recv.at[step],
            device_id={"seq": mate},
            device_id_type=MESH,
        )

    def keep_bit(stage):
        return lax.rem(lax.div(level, 2**stage), 2)

    def partner(stage):
        return me + 2 ** (stage + 1) * (1 - 2 * keep_bit(stage))

    def part_of(stage, place):
        low = lax.rem(level, 2**stage)
        return low + 2**stage * (1 - keep_bit(stage)) + 2 ** (stage + 1) * place

    def far_slot(stage, part):
        return outer - outer // 2**stage + lax.div(part, 2 ** (stage + 1))

    def far_copy(stage, part):
        slot = far_slot(stage, part)
        return pltpu.make_async_remote_copy(
            src_ref=far_out.at[part],
            dst_ref=far_in.at[slot],
            send_sem=far_send.at[part],
            recv_sem=far_recv.at[slot],
            device_id={"seq": partner(stage)},
            device_id_type=MESH,
        )

    def half_rows(half):
        return pl.ds(half * half_share, half_share)

    def half_pair_copy(half, step):
        return pltpu.make_async_remote_copy(
            src_ref=pair_out.at[step, half_rows(half)],
            dst_ref=pair_in.at[step, half_rows(half)],
            send_sem=half_pair_send.at[half, step],
            recv_sem=half_pair_recv.at[half, step],
            device_id={"seq": mate},
            device_id_type=MESH,
        )

    def half_far_copy(half, stage, part):
        slot = far_slot(stage, part)
        return pltpu.make_async_remote_copy(
            src_ref=far_out.at[part, half_rows(half)],
            dst_ref=far_in.at[slot, half_rows(half)],
            send_sem=half_far_send.at[half, part],
            recv_sem=half_far_recv.at[half, slot],
            device_id={"seq": partner(stage)},
            device_id_type=MESH,
        )

    def flat_rows(step, which):
        return pl.ds(pl.multiple_of((2 * step + which) * share, 16), share)

    def flat_half(step, which, half):
        at = (2 * step + which) * share + half * half_share
        return pl.ds(pl.multiple_of(at, 8), half_share)

    def pair_start(step, carry):
        pair_out[step] = flat[flat_rows(step, 1 - side), :].astype(BF16)
        pair_copy(step).start()
        return carry

    def part_sum(stage, part):
        pair_copy(part).wait_recv()
        total = flat[flat_rows(part, side), :] + pair_in[part].astype(F32)
        for before in range(stage):
            far_copy(before, part).wait_recv()
            total = total + far_in[far_slot(before, part)].astype(F32)
        return total

    def far_start(stage, first, last):
        def start(place, carry):
            part = part_of(stage, place)

            @pl.when(jnp.logical_and(part >= first, part < last))
            def _():
                far_out[part] = part_sum(stage, part).astype(BF16)
                far_copy(stage, part).start()

            return carry

        lax.fori_loop(0, outer // 2 ** (stage + 1), start, 0)

    def half_grad(half):
        for col in range(half, cols_qkv, 2):
            grad = mm_t(normed_s[...], d_packed_s[col * LANES : (col + 1) * LANES, :])
            for shard in range(2 * late):
                at = shard * share + half * half_share + (col // 2) * slab
                flat[at : at + slab, :] = grad[shard * slab : (shard + 1) * slab]

    def half_pair_start(half):
        def start(step, carry):
            pair_out[step, half_rows(half)] = flat[flat_half(step, 1 - side, half), :].astype(BF16)
            half_pair_copy(half, step).start()
            return carry

        lax.fori_loop(0, late, start, 0)

    def half_sum(half, stage, part):
        half_pair_copy(half, part).wait_recv()
        total = flat[flat_half(part, side, half), :]
        total = total + pair_in[part, half_rows(half)].astype(F32)
        for before in range(stage):
            half_far_copy(half, before, part).wait_recv()
            total = total + far_in[far_slot(before, part), half_rows(half)].astype(F32)
        return total

    def half_far_start(half, stage):
        def start(place, carry):
            part = part_of(stage, place)

            @pl.when(part < late)
            def _():
                far_out[part, half_rows(half)] = half_sum(half, stage, part).astype(BF16)
                half_far_copy(half, stage, part).start()

            return carry

        lax.fori_loop(0, outer // 2 ** (stage + 1), start, 0)

    land_all(1)
    upstream = mm(jnp.transpose(arrived(1)), land_sel[...])
    branch = (keep * upstream).astype(BF16)
    spread_flat(at_down, mm_t(act_s[...], branch))
    lax.fori_loop(ready, outer, pair_start, 0)
    block = hidden_s[...].astype(F32) + keep * mm(w_down_t[...], act_s[...])
    fill(2, mm_t(land_sel[...], block.astype(BF16)))
    send_all(2)

    def down_piece(step, carry):
        at = pl.multiple_of(step * piece, piece)
        d_act = mm(w_down[pl.ds(at, piece), :], branch)
        pre = slope_s[pl.ds(at, piece), :]
        square = pre * pre
        curve = jnp.tanh(inner * (pre + 0.044715 * square * pre))
        bend = 0.5 * (1.0 - curve * curve) * (inner * (1.0 + 3.0 * 0.044715 * square))
        slope = 0.5 * (1.0 + curve) + pre * bend
        act_s[pl.ds(at, piece), :] = (d_act * slope).astype(BF16)
        return carry

    lax.fori_loop(0, hid // piece, down_piece, 0)
    spread_flat(at_up, mm_t(normed_two_s[...], act_s[...]))
    d_hidden = upstream + norm_back(hidden_s[...].astype(F32), mm(w_up[...], act_s[...]))
    d_hidden_s[...] = d_hidden.astype(BF16)
    branch_one = (keep * d_hidden_s[...].astype(F32)).astype(BF16)
    spread_flat(at_out, mm_t(mixed_s[...], branch_one))
    d_mixed_s[...] = mm(w_out[...], branch_one).astype(BF16)

    def head_backward(head):
        at = pl.multiple_of(head * depth, depth)
        query = packed_s[pl.ds(at, depth), :] * jnp.asarray(factor, BF16)
        keys = packed_s[pl.ds(chans + at, depth), :]
        values = packed_s[pl.ds(2 * chans + at, depth), :]
        values_more = jnp.transpose(jnp.concatenate([values, two_rows], axis=0))
        scaled = (d_mixed_s[pl.ds(at, depth), :].astype(F32) * inverse_s[head]).astype(BF16)
        mixed = mixed_s[pl.ds(at, depth), :].astype(F32)
        delta = -jnp.sum(scaled.astype(F32) * mixed, axis=0, keepdims=True)
        coarse = delta.astype(BF16).astype(F32)
        fine = delta - coarse
        tail = jnp.where(
            row_ids == 0,
            jnp.broadcast_to(coarse, (depth, rows)),
            jnp.where(row_ids == 1, jnp.broadcast_to(fine, (depth, rows)), 0.0),
        ).astype(BF16)
        scaled_more = jnp.concatenate([scaled, tail], axis=0)
        weights = weights_s[head]
        gap = mm(values_more, scaled_more).astype(BF16)
        d_scores = weights * gap
        d_query = mm(keys, d_scores) * factor
        d_packed_s[pl.ds(at, depth), :] = d_query.astype(BF16)
        d_packed_s[pl.ds(chans + at, depth), :] = mm_t(query, d_scores).astype(BF16)
        d_packed_s[pl.ds(2 * chans + at, depth), :] = mm_t(scaled, weights).astype(BF16)

    lax.fori_loop(late, ready, pair_start, 0)

    bunches = heads // bunch

    groups = ((ready, outer), (middle, ready), (late, middle))

    def relay(place):
        for stage, group in PLAN.get(place, ()):
            for step in (stage,) if stage == 0 else range(stage, stages):
                if group < len(groups):
                    first, last = groups[group]
                    if first < last:
                        far_start(step, first, last)
                else:
                    half_far_start(group - len(groups), step)

    def backward_bunch(step, carry):
        for place in range(bunch):
            head_backward(bunch * step + place)
        for place in range(bunches):
            if place in PLAN:

                @pl.when(step == place)
                def _(place=place):
                    relay(place)

        @pl.when(step == bunches // 2 - 1)
        def _():
            half_grad(0)
            half_pair_start(0)

        return carry

    lax.fori_loop(0, bunches, backward_bunch, 0)
    half_grad(1)
    half_pair_start(1)
    relay(BEFORE_LAST)
    d_moved = d_hidden_s[...].astype(F32) + norm_back(
        moved_s[...].astype(F32), mm(w_qkv[...], d_packed_s[...])
    )
    fill(3, mm_t(land_sel[...], d_moved.astype(BF16)))
    send_all(3)
    relay(AFTER_LAST)

    land_all(2)
    out_feats[...] = mm(unpack_sel[...], arrived(2)).astype(BF16)

    relay(AT_END)

    land_all(3)
    grad_feats[...] = mm(unpack_sel[...], arrived(3)).astype(BF16)

    @pl.when(level >= late)
    def _():
        weight_grads[...] = part_sum(stages, level)

    @pl.when(level < late)
    def _():
        for half in range(2):
            flat[flat_half(level, side, half), :] = half_sum(half, stages, level)
        for col in range(cols_qkv):
            at = (2 * level + side) * share + (col % 2) * half_share + (col // 2) * slab
            weight_grads[pl.ds(col, slab, stride=cols_qkv), :] = flat[
                pl.ds(pl.multiple_of(at, 8), slab), :
            ]

    def pair_drain(step, carry):
        pair_copy(step).wait_send()
        return carry

    lax.fori_loop(late, outer, pair_drain, 0)

    def far_drain(stage):
        def wait(place, carry):
            part = part_of(stage, place)

            @pl.when(part >= late)
            def _():
                far_copy(stage, part).wait_send()

            @pl.when(part < late)
            def _():
                for half in range(2):
                    half_far_copy(half, stage, part).wait_send()

            return carry

        lax.fori_loop(0, outer // 2 ** (stage + 1), wait, 0)

    for stage in range(stages):
        far_drain(stage)

    def half_drain(step, carry):
        for half in range(2):
            half_pair_copy(half, step).wait_send()
        return carry

    lax.fori_loop(0, late, half_drain, 0)
    for which in range(4):
        drain(which)


def hand_over(*refs):
    count = (len(refs) - 2) // 3
    sources, targets, helds = (refs[count * place : count * (place + 1)] for place in range(3))
    load_sem, store_sem = refs[3 * count :]
    loads = [
        pltpu.make_async_copy(sources[place], helds[place], load_sem.at[place])
        for place in range(count)
    ]
    stores = [
        pltpu.make_async_copy(helds[place], targets[place], store_sem.at[place])
        for place in range(count)
    ]
    for load in loads:
        load.start()
    for load, store in zip(loads, stores):
        load.wait()
        store.start()
    for store in stores:
        store.wait()


def body(feats, cotangent, w_qkv, w_out, w_up, w_down, hilbert_src, z_dest, valid_count):
    rows, chans = feats.shape
    hid = w_up.shape[1]
    shards = lax.axis_size("seq")
    slots = 2 * rows // shards
    outer = shards // 2
    packed = w_qkv.shape[1]
    flat_rows = (chans * packed + chans * chans + 2 * chans * hid) // LANES
    share = flat_rows // shards
    vmem = pl.BlockSpec(memory_space=pltpu.VMEM)
    dma = pltpu.SemaphoreType.DMA
    out_feats, grad_feats, weight_grads = pl.pallas_call(
        functools.partial(kernel, shards, slots),
        out_shape=(
            jax.ShapeDtypeStruct((rows, chans), BF16),
            jax.ShapeDtypeStruct((rows, chans), BF16),
            jax.ShapeDtypeStruct((share, LANES), F32),
        ),
        in_specs=[pl.BlockSpec(memory_space=pltpu.HBM)] * 9,
        out_specs=(vmem, vmem, vmem),
        scratch_shapes=[
            pltpu.VMEM((4, shards, slots, chans), BF16),
            pltpu.VMEM((4, shards, slots, chans), BF16),
            pltpu.VMEM((shards * slots, rows), BF16),
            pltpu.VMEM((rows, shards * slots), BF16),
            pltpu.VMEM((shards * slots, rows), BF16),
            pltpu.VMEM((packed, chans), BF16),
            pltpu.VMEM((chans, chans), BF16),
            pltpu.VMEM((hid, chans), BF16),
            pltpu.VMEM((chans, hid), BF16),
            pltpu.VMEM((chans, rows), BF16),
            pltpu.VMEM((chans, rows), BF16),
            pltpu.VMEM((packed, rows), BF16),
            pltpu.VMEM((chans, rows), BF16),
            pltpu.VMEM((chans, rows), BF16),
            pltpu.VMEM((chans, rows), BF16),
            pltpu.VMEM((hid, rows), BF16),
            pltpu.VMEM((hid, rows), F32),
            pltpu.VMEM((HEADS, rows, rows), BF16),
            pltpu.VMEM((HEADS, 1, rows), F32),
            pltpu.VMEM((chans, rows), BF16),
            pltpu.VMEM((chans, rows), BF16),
            pltpu.VMEM((packed, rows), BF16),
            pltpu.VMEM((flat_rows, LANES), F32),
            pltpu.VMEM((outer, share, LANES), BF16),
            pltpu.VMEM((outer, share, LANES), BF16),
            pltpu.VMEM((outer, share, LANES), BF16),
            pltpu.VMEM((outer, share, LANES), BF16),
            dma((4, shards)),
            dma((4, shards)),
            dma((outer,)),
            dma((outer,)),
            dma((outer,)),
            dma((outer,)),
            dma((2, outer)),
            dma((2, outer)),
            dma((2, outer)),
            dma((2, outer)),
            pltpu.VMEM((rows, chans), BF16),
            pltpu.VMEM((rows, chans), BF16),
            pltpu.VMEM((chans, packed), BF16),
            pltpu.VMEM((chans, chans), BF16),
            pltpu.VMEM((chans, hid), BF16),
            pltpu.VMEM((hid, chans), BF16),
            pltpu.VMEM((1, rows), jnp.int32),
            pltpu.VMEM((1, rows), jnp.int32),
            pltpu.SMEM((1,), jnp.int32),
            dma((9,)),
        ],
        compiler_params=pltpu.CompilerParams(
            collective_id=0, has_side_effects=True, vmem_limit_bytes=60 * 1024 * 1024
        ),
        name="block_step",
    )(
        feats,
        cotangent,
        w_qkv,
        w_out,
        w_up,
        w_down,
        hilbert_src.reshape(1, rows),
        z_dest.reshape(1, rows),
        valid_count,
    )
    results = (out_feats, grad_feats, weight_grads)
    far = pl.BlockSpec(memory_space=pltpu.HBM)
    out_feats, grad_feats, weight_grads = pl.pallas_call(
        hand_over,
        out_shape=tuple(jax.ShapeDtypeStruct(array.shape, array.dtype) for array in results),
        in_specs=[far] * len(results),
        out_specs=(far,) * len(results),
        scratch_shapes=[pltpu.VMEM(array.shape, array.dtype) for array in results]
        + [dma((len(results),)), dma((len(results),))],
        name="hand_over",
    )(*results)
    return out_feats, grad_feats, weight_grads.reshape(-1)


def solution(mesh):
    in_specs = (
        P(("dp", "seq"), None),
        P(("dp", "seq"), None),
        P(),
        P(),
        P(),
        P(),
        P(("dp", "seq")),
        P(("dp", "seq")),
        P(("dp", "seq")),
    )
    out_specs = (P(("dp", "seq"), None), P(("dp", "seq"), None), P(("dp", "seq")))
    return jax.shard_map(body, mesh=mesh, in_specs=in_specs, out_specs=out_specs, check_vma=False)
```
